512 devices in a mesh: dp: 16 (over z, core), expert: 32 (over x, y).
Axes of the slice: x: 4, y: 8, z: 8, core: 2. Of those that a mesh axis runs over, the one named last changes fastest.
Arguments:
- pivot_states: bfloat16 [65536, 2048], P(('dp', 'expert')), may hold values from -6 to 6
- queries: bfloat16 [65536, 2048], P(('dp', 'expert')), may hold values from -8 to 8
- keys: bfloat16 [65536, 2048], P(('dp', 'expert')), may hold values from -8 to 8
- values: bfloat16 [65536, 2048], P(('dp', 'expert')), may hold values from -6 to 6
- pack_pos: int32 [65536], P(('dp', 'expert')), may hold values from 0 to 2047, as said below
- segment_ids: int32 [512, 128], P(('dp', 'expert')), may hold values from 0 to 7, never falling along the last dimension, each value on 1 to 64 neighbouring positions
- expert_ids: int32 [65536, 2], P(('dp', 'expert')), may hold values from 0 to 127, all different within a row
- gate_code: int32 [65536, 2], P(('dp', 'expert')), may hold values from 6554 to 65535
- ln_gain: float32 [2048], replicated, may hold values from 0.5 to 1.5
- ln_bias: float32 [2048], replicated, may hold values from -3 to 3
- w_in: bfloat16 [32, 2048, 4096], P('expert', None, 'dp'), may hold values from -0.125 to 0.125
- b_in: float32 [32, 4096], P('expert', 'dp'), may hold values from -3 to 3
- w_out: bfloat16 [32, 4096, 2048], P('expert', 'dp'), may hold values from -0.09375 to 0.09375
- b_out: float32 [32, 2048], replicated, may hold values from -3 to 3
Outputs:
- layer_out: bfloat16 [65536, 2048], P(('dp', 'expert'))
The draws below stay inside these ranges and needn't reach their ends.
Inputs may be any that keep to these rules, and one draw needn't show every extreme that they name: Within one index of expert, pack_pos over the devices of dp is a permutation, and each device's tokens go exactly 8 to each packed block of its column. `expert_ids`: only ids below 32 belong to the experts of this round.
All inputs are finite; a program needn't handle non-finite values.
Results may differ from the reference program's by a relative error of at most 0.0055.
Values may be sent and summed in bfloat16 or wider, within the bound.
A program may use at most 64 MiB of HBM per device.

```python
import math
import jax
import jax.numpy as jnp
import numpy as np
from jax import lax

D = 2048
HEAD_DIM = 128
FF = 4096
TOK_DEV = 128
EXPERTS = 32
EXPERTS_ALL = 128
CAP = 2
BLOCKS = 512
TOKENS = 65536
N_DP = 16
N_EXPERT = 32


def drawn_rows(key, offset_tag):
    gaussian = jax.random.normal(jax.random.fold_in(key, offset_tag), (TOKENS, D), jnp.float32)
    return jnp.clip(gaussian, -6.0, 6.0)


def draw_queries(key, part):
    return drawn_rows(key, 3).astype(jnp.bfloat16)


def draw_keys(key, part):
    return drawn_rows(key, 5).astype(jnp.bfloat16)


def draw_pack_pos(key, part):
    per_target = TOK_DEV // N_DP
    first_key = jax.random.fold_in(key, 101)
    second_key = jax.random.fold_in(key, 202)
    target_keys = jax.random.split(first_key, N_EXPERT * N_DP)
    target_perm = jax.vmap(lambda subkey: jax.random.permutation(subkey, TOK_DEV))(target_keys)
    target_perm = target_perm.reshape(N_EXPERT, N_DP, TOK_DEV)
    source_keys = jax.random.split(second_key, N_DP * N_EXPERT)
    send_order = jax.vmap(lambda subkey: jax.random.permutation(subkey, TOK_DEV))(source_keys)
    send_order = send_order.reshape(N_DP, N_EXPERT, TOK_DEV)
    target_block = send_order // per_target
    within_share = send_order % per_target
    source_row = jnp.arange(N_DP, dtype=jnp.int32)[:, None, None]
    column_row = jnp.arange(N_EXPERT, dtype=jnp.int32)[None, :, None]
    offsets = target_perm[column_row, target_block, source_row * per_target + within_share]
    return (target_block * TOK_DEV + offsets).astype(jnp.int32).reshape(TOKENS)


def place_ends(values, key, smallest, largest):
    spot = [jax.random.randint(jax.random.fold_in(key, axis), (), 0, length) for axis, length in enumerate(values.shape)]
    widest = values.shape.index(max(values.shape))
    beside = spot[:widest] + [(spot[widest] + 1) % values.shape[widest]] + spot[widest + 1:]
    return values.at[tuple(spot)].set(smallest).at[tuple(beside)].set(largest)


def block_scale(own_key, shape, cuts, least, top_value):
    factor_of = 1.0
    for position, shards_of in cuts:
        steps = jax.random.uniform(jax.random.fold_in(jax.random.fold_in(own_key, 6), position), (shards_of,), jnp.float32, least / len(cuts), top_value / len(cuts))
        factor_of = factor_of * jnp.repeat(jnp.exp(steps), shape[position] // shards_of).reshape((-1,) + (1,) * (len(shape) - 1 - position))
    return factor_of


def different_ones(key, rows, amount, top, lift):
    order = jax.random.permutation(jax.random.fold_in(key, 1), amount)
    boost = order
    for power in range(3):
        boost = boost * boost // amount
    boost = boost * lift // amount
    chance = jax.random.randint(jax.random.fold_in(key, 2), (rows, amount), 0, 4096) + boost
    fixed_rows = jax.random.permutation(jax.random.fold_in(key, 3), rows)[jnp.arange(amount) % rows]
    chance = jnp.where(jnp.arange(rows)[:, None] == fixed_rows[None, :], 1 << 14, chance)
    merit = chance * amount + jnp.arange(amount)
    return lax.top_k(merit.astype(jnp.int32), top)[1].astype(jnp.int32)


def length_profile(number_of, total, bound, skew):
    loads = [(1 << 20) // math.isqrt(grade ** skew) + 1 for grade in range(2, number_of + 1)]
    surplus, holding = total - bound - (number_of - 1), [1] * (number_of - 1)
    while surplus > 0:
        candidates = [i for i in range(number_of - 1) if holding[i] < bound]
        pool, remaining = sum([loads[i] for i in candidates]), surplus
        for i in candidates:
            more = min(bound - holding[i], max(1, remaining * loads[i] // pool), surplus)
            holding[i] = holding[i] + more
            surplus = surplus - more
    return np.array([bound] + holding)


def uneven(key, count, total, most, skew):
    if count == 2:
        one = jax.random.randint(key, (), max(1, total - most), min(most, total - 1) + 1)
        return jnp.stack([one, total - one])
    tallies = jnp.asarray(length_profile(count, total, most, skew), jnp.int32)
    couples = (count - 1) // 2
    giver, receiver = tallies[1:1 + 2 * couples:2], tallies[2:2 + 2 * couples:2]
    room = jnp.minimum(giver - 1, most - receiver)
    passed = jax.random.randint(jax.random.fold_in(key, 1), (couples,), 0, 1 << 20) % (room + 1)
    tallies = tallies.at[1:1 + 2 * couples:2].set(giver - passed).at[2:2 + 2 * couples:2].set(receiver + passed)
    return tallies[jax.random.permutation(jax.random.fold_in(key, 2), count)]


def centred(stream_key, dims, spread, reach, shards=(), kind=jnp.bfloat16):
    values = spread * jax.random.normal(stream_key, dims, jnp.float32)
    if shards:
        values = values * block_scale(stream_key, dims, shards, -0.22, 0.18)
    return jnp.clip(values, -reach, reach).astype(kind)


def setup_inputs(seed: int = 0) -> dict:
    key_list = jax.random.split(jax.random.key(seed), 15)
    return {
        "pivot_states": centred(key_list[0], (TOKENS, D), 1.0, 6.0, ((0, 512),)),
        "queries": draw_queries(jax.random.fold_in(key_list[14], 71), 0),
        "keys": draw_keys(jax.random.fold_in(key_list[14], 71), 0),
        "values": centred(key_list[3], (TOKENS, D), 1.0, 6.0, ((0, 512),)),
        "pack_pos": draw_pack_pos(jax.random.fold_in(key_list[14], 71), 0),
        "segment_ids": jax.vmap(lambda own: jnp.searchsorted(jnp.cumsum(uneven(own, TOK_DEV // 16, TOK_DEV, TOK_DEV // 2, 2)), jnp.arange(TOK_DEV), side="right"))(jax.random.split(key_list[5], BLOCKS)).reshape((BLOCKS, TOK_DEV)).astype(jnp.int32),
        "expert_ids": different_ones(key_list[6], TOKENS, EXPERTS_ALL, 2, 256),
        "gate_code": place_ends(jax.random.randint(key_list[7], (TOKENS, 2), 6554, 65536), jax.random.fold_in(key_list[7], 1), 6554, 65535).astype(jnp.int32),
        "ln_gain": jnp.clip(1.0 + 0.1 * jax.random.normal(key_list[8], (D,), jnp.float32), 0.5, 1.5),
        "ln_bias": centred(key_list[9], (D,), 0.5, 3.0, (), jnp.float32),
        "w_in": centred(key_list[10], (EXPERTS, D, FF), D ** -0.5, 0.125, ((0, 32), (2, 16))),
        "b_in": centred(key_list[11], (EXPERTS, FF), 0.5, 3.0, ((0, 32), (1, 16)), jnp.float32),
        "w_out": centred(key_list[12], (EXPERTS, FF, D), FF ** -0.5, 0.09375, ((0, 32), (1, 16))),
        "b_out": centred(key_list[13], (EXPERTS, D), 0.5, 3.0, (), jnp.float32),
    }


epsilon = 1e-05
mask_fill = -1e+30

def attend_block(block_args):
    query_rows, key_rows, value_rows, seg_row = block_args
    row_count = query_rows.shape[0]
    head_count = query_rows.shape[1] // HEAD_DIM
    query_heads = query_rows.astype(jnp.float32).reshape(row_count, head_count, HEAD_DIM)
    key_heads = key_rows.astype(jnp.float32).reshape(row_count, head_count, HEAD_DIM)
    value_heads = value_rows.astype(jnp.float32).reshape(row_count, head_count, HEAD_DIM)
    scores = jnp.einsum('qhd,khd->hqk', query_heads, key_heads) * (1.0 / math.sqrt(HEAD_DIM))
    same_doc = seg_row[:, None] == seg_row[None, :]
    scores = jnp.where(same_doc[None, :, :], scores, mask_fill)
    top_score = lax.optimization_barrier(jnp.max(scores, axis=2, keepdims=True))
    exp_terms = jnp.exp(scores - top_score)
    softmax_weights = (exp_terms / lax.optimization_barrier(jnp.sum(exp_terms, axis=2, keepdims=True))).astype(jnp.bfloat16)
    attended = jnp.einsum('hqk,khd->qhd', softmax_weights.astype(jnp.float32), value_heads)
    return attended.reshape(row_count, head_count * HEAD_DIM)

def expert_apply(expert_args):
    rows_in, first_matrix, bias_in, second_matrix, bias_out = expert_args
    hidden_units = first_matrix.shape[1] // N_DP
    running_total = jnp.zeros((rows_in.shape[0], second_matrix.shape[1]), jnp.float32)
    for slice_index in range(N_DP):
        lower_edge = slice_index * hidden_units
        hidden = jnp.dot(rows_in, first_matrix[:, lower_edge:lower_edge + hidden_units], preferred_element_type=jnp.float32)
        hidden = jnp.maximum(hidden + bias_in[lower_edge:lower_edge + hidden_units], 0.0).astype(jnp.bfloat16)
        partial_share = jnp.dot(hidden, second_matrix[lower_edge:lower_edge + hidden_units], preferred_element_type=jnp.float32).astype(jnp.bfloat16)
        partial_share = lax.optimization_barrier(partial_share)
        running_total = running_total + partial_share.astype(jnp.float32)
    return (running_total + bias_out).astype(jnp.bfloat16)

def reference(pivot_states, queries, keys, values, pack_pos, segment_ids, expert_ids, gate_code, ln_gain, ln_bias, w_in, b_in, w_out, b_out):
    tokens_all = pivot_states.shape[0]
    model_width = pivot_states.shape[1]
    blocks_all = tokens_all // TOK_DEV
    source_index = jnp.arange(tokens_all, dtype=jnp.int32)
    column_index = source_index // TOK_DEV % N_EXPERT
    destination = (pack_pos // TOK_DEV * N_EXPERT + column_index) * TOK_DEV + pack_pos % TOK_DEV

    def regroup(array):
        return jnp.zeros_like(array).at[destination].set(array)
    states_packed = regroup(pivot_states)
    attended = lax.map(attend_block, (regroup(queries).reshape(blocks_all, TOK_DEV, model_width), regroup(keys).reshape(blocks_all, TOK_DEV, model_width), regroup(values).reshape(blocks_all, TOK_DEV, model_width), segment_ids))
    hidden_state = states_packed.astype(jnp.float32) + attended.reshape(tokens_all, model_width)
    mean_value = lax.optimization_barrier(jnp.mean(hidden_state, axis=1, keepdims=True))
    centered = hidden_state - mean_value
    variance = lax.optimization_barrier(jnp.mean(centered * centered, axis=1, keepdims=True))
    normed = (centered * lax.rsqrt(variance + epsilon) * ln_gain + ln_bias).astype(jnp.bfloat16)
    experts_round = N_EXPERT
    choice_ids = expert_ids.reshape(blocks_all, TOK_DEV, 2)
    assigned = jnp.concatenate([choice_ids[:, :, 0], choice_ids[:, :, 1]], axis=1)
    expert_hot = (assigned[:, :, None] == jnp.arange(experts_round, dtype=jnp.int32)[None, None, :]).astype(jnp.int32)
    slot_rank = lax.optimization_barrier(jnp.sum(jnp.cumsum(expert_hot, axis=1) * expert_hot, axis=2)) - 1
    kept_mask = (assigned < experts_round) & (slot_rank < CAP)
    block_index = jnp.arange(blocks_all, dtype=jnp.int32)[:, None]
    overflow = experts_round * blocks_all * CAP
    slot_index = jnp.where(kept_mask, (assigned * blocks_all + block_index) * CAP + slot_rank, overflow).astype(jnp.int32)
    slot_first = slot_index[:, :TOK_DEV].reshape(tokens_all)
    slot_second = slot_index[:, TOK_DEV:].reshape(tokens_all)
    buffer = jnp.zeros((overflow, model_width), jnp.bfloat16)
    buffer = buffer.at[slot_first].set(normed, mode='drop').at[slot_second].set(normed, mode='drop')
    results = lax.map(expert_apply, (buffer.reshape(experts_round, blocks_all * CAP, model_width), w_in, b_in, w_out, b_out))
    results = results.reshape(overflow, model_width)
    gate_values = gate_code.astype(jnp.float32) / 65536.0
    weight_first = jnp.where(kept_mask[:, :TOK_DEV].reshape(tokens_all), gate_values[:, 0], 0.0)
    weight_second = jnp.where(kept_mask[:, TOK_DEV:].reshape(tokens_all), gate_values[:, 1], 0.0)
    picked_first = results[jnp.minimum(slot_first, overflow - 1)].astype(jnp.float32)
    picked_second = results[jnp.minimum(slot_second, overflow - 1)].astype(jnp.float32)
    layer_out = hidden_state + weight_first[:, None] * picked_first + weight_second[:, None] * picked_second
    return layer_out.astype(jnp.bfloat16)
```

```python
import math

import jax
import jax.numpy as jnp
from jax import lax
from jax.experimental import pallas as pl
from jax.experimental.pallas import tpu as pltpu
from jax.sharding import PartitionSpec as P

HEAD_DIM = 128
ROUNDS = 4


epsilon = 1e-05
mask_fill = -1e30


MESH_ID = pl.DeviceIdType.MESH


def expert_kernel(
    x_ref,
    w1_ref,
    b1_ref,
    w2_ref,
    b2_ref,
    o_ref,
    rows,
    part,
    pair_in,
    run_out,
    run_in,
    w1_v,
    w2_v,
    load_sem,
    ag_send,
    ag_recv,
    sib_send,
    sib_recv,
    pair_send,
    pair_recv,
    run_send,
    run_recv,
):
    chips = lax.axis_size("dp") // 2
    me = lax.axis_index("dp")
    z = me // 2
    core = me % 2
    ahead = ((z + 1) % chips) * 2 + core
    behind = ((z + chips - 1) % chips) * 2 + core
    sibling = z * 2 + 1 - core
    half, width = rows.shape[3], rows.shape[4]
    steps = chips

    loads = (
        pltpu.make_async_copy(x_ref, rows.at[0, 0], load_sem.at[0]),
        pltpu.make_async_copy(w1_ref.at[0], w1_v, load_sem.at[1]),
        pltpu.make_async_copy(w2_ref.at[0], w2_v, load_sem.at[2]),
    )
    for load in loads:
        load.start()
    barrier = pltpu.get_barrier_semaphore()
    for peer in (ahead, behind, sibling):
        pl.semaphore_signal(barrier, inc=1, device_id={"dp": peer}, device_id_type=MESH_ID)
    pl.semaphore_wait(barrier, 3)
    loads[0].wait()

    def pass_on(s, way):
        return pltpu.make_async_remote_copy(
            src_ref=rows.at[s, 0, way],
            dst_ref=rows.at[s + 1, 0, way],
            send_sem=ag_send.at[s, way],
            recv_sem=ag_recv.at[s, way],
            device_id={"dp": (ahead, behind)[way]},
            device_id_type=MESH_ID,
        )

    def to_sibling(s):
        return pltpu.make_async_remote_copy(
            src_ref=rows.at[s, 0],
            dst_ref=rows.at[s, 1],
            send_sem=sib_send.at[s],
            recv_sem=sib_recv.at[s],
            device_id={"dp": sibling},
            device_id_type=MESH_ID,
        )

    def pair(s):
        return pltpu.make_async_remote_copy(
            src_ref=part.at[s, 1],
            dst_ref=pair_in.at[s],
            send_sem=pair_send.at[s],
            recv_sem=pair_recv.at[s],
            device_id={"dp": sibling},
            device_id_type=MESH_ID,
        )

    def run(s, way):
        return pltpu.make_async_remote_copy(
            src_ref=run_out.at[s - 1, way],
            dst_ref=run_in.at[s - 1, way],
            send_sem=run_send.at[s - 1, way],
            recv_sem=run_recv.at[s - 1, way],
            device_id={"dp": (ahead, behind)[way]},
            device_id_type=MESH_ID,
        )

    def step(i, carry):
        @pl.when(i < steps)
        def _():
            @pl.when(i >= 1)
            def _():
                for way in range(2):
                    pass_on(i - 1, way).wait_recv()

            @pl.when(i < steps - 1)
            def _():
                for way in range(2):
                    pass_on(i, way).start()

            to_sibling(i).start()

        @pl.when(i == 1)
        def _():
            loads[1].wait()
            loads[2].wait()

        @pl.when((i >= 1) & (i <= steps))
        def _():
            s = i - 1
            to_sibling(s).wait_recv()
            held = rows[s].reshape(4 * half, width)
            hidden = jnp.dot(held, w1_v[...], preferred_element_type=jnp.float32)
            hidden = jnp.maximum(hidden + b1_ref[...], 0.0).astype(jnp.bfloat16)
            share = jnp.dot(hidden, w2_v[...], preferred_element_type=jnp.float32)
            part[s] = share.astype(jnp.bfloat16).reshape(2, 2, half, width)
            pair(s).start()

        @pl.when(i == 3)
        def _():
            pair(1).wait_recv()
            total = part[1, 0].astype(jnp.float32) + pair_in[1].astype(jnp.float32)
            run_out[0] = total.astype(jnp.bfloat16)
            for way in range(2):
                run(1, way).start()

        @pl.when(i > 3)
        def _():
            s = i - 2
            pair(s).wait_recv()
            total = part[s, 0].astype(jnp.float32) + pair_in[s].astype(jnp.float32)
            for way in range(2):
                run(s - 1, way).wait_recv()
            total = total + run_in[s - 2].astype(jnp.float32)
            run_out[s - 1] = total.astype(jnp.bfloat16)
            for way in range(2):
                run(s, way).start()

        return carry

    lax.fori_loop(0, steps + 2, step, 0)
    pair(0).wait_recv()
    total = part[0, 0].astype(jnp.float32) + pair_in[0].astype(jnp.float32)
    total = total + b2_ref[pl.ds(lax.axis_index("expert"), 1), :].reshape(1, 1, width)
    for way in range(2):
        run(steps - 1, way).wait_recv()
    total = total + run_in[steps - 2].astype(jnp.float32)
    o_ref[...] = total.astype(jnp.bfloat16).reshape(2 * half, width)

    def drain(s, carry):
        to_sibling(s).wait_send()
        pair(s).wait_send()

        @pl.when(s < steps - 1)
        def _():
            for way in range(2):
                pass_on(s, way).wait_send()
                run(s + 1, way).wait_send()

        return carry

    lax.fori_loop(0, steps, drain, 0)


def experts(arrived, w_in, b_in, w_out, b_out):
    count, width = arrived.shape
    units = w_in.shape[2]
    half = count // 2
    chips = lax.axis_size("dp") // 2
    dma = pltpu.SemaphoreType.DMA
    bf16 = jnp.bfloat16
    any_space = pl.BlockSpec(memory_space=pl.ANY)
    vmem = pl.BlockSpec(memory_space=pltpu.VMEM)
    return pl.pallas_call(
        expert_kernel,
        out_shape=jax.ShapeDtypeStruct((count, width), bf16),
        in_specs=[any_space, any_space, vmem, any_space, vmem],
        out_specs=vmem,
        scratch_shapes=[
            pltpu.VMEM((chips, 2, 2, half, width), bf16),
            pltpu.VMEM((chips, 2, 2, half, width), bf16),
            pltpu.VMEM((chips, 2, half, width), bf16),
            pltpu.VMEM((chips - 1, 2, half, width), bf16),
            pltpu.VMEM((chips - 1, 2, half, width), bf16),
            pltpu.VMEM((width, units), bf16),
            pltpu.VMEM((units, width), bf16),
            dma((3,)),
            dma((chips - 1, 2)),
            dma((chips - 1, 2)),
            dma((chips,)),
            dma((chips,)),
            dma((chips,)),
            dma((chips,)),
            dma((chips - 1, 2)),
            dma((chips - 1, 2)),
        ],
        compiler_params=pltpu.CompilerParams(collective_id=1, has_side_effects=True),
        name="expert_ring",
    )(arrived.reshape(2, half, width), w_in, b_in, w_out, b_out)


def per_device(
    pivot_states,
    queries,
    keys,
    values,
    pack_pos,
    segment_ids,
    expert_ids,
    gate_code,
    ln_gain,
    ln_bias,
    w_in,
    b_in,
    w_out,
    b_out,
):
    tok_count = pivot_states.shape[0]
    model_width = pivot_states.shape[1]
    dp_count = lax.axis_size("dp")
    expert_count = lax.axis_size("expert")
    per_target = tok_count // dp_count
    target_block = pack_pos // tok_count
    offsets = pack_pos % tok_count
    target_hot = (target_block[:, None] == jnp.arange(dp_count, dtype=jnp.int32)[None, :]).astype(
        jnp.int32
    )
    bucket_rank = jnp.sum(jnp.cumsum(target_hot, axis=0) * target_hot, axis=1) - 1
    send_index = target_block * per_target + bucket_rank
    joined = jnp.concatenate([pivot_states, queries, keys, values], axis=1)
    send_rows = jnp.zeros_like(joined).at[send_index].set(joined)
    send_offsets = jnp.zeros_like(offsets).at[send_index].set(offsets)
    recv_rows, recv_offsets = (
        lax.all_to_all(send_rows, "dp", split_axis=0, concat_axis=0, tiled=True),
        lax.all_to_all(send_offsets, "dp", split_axis=0, concat_axis=0, tiled=True),
    )
    packed = jnp.zeros_like(recv_rows).at[recv_offsets].set(recv_rows)
    state_rows = packed[:, :model_width]
    query_rows = packed[:, model_width : 2 * model_width]
    key_rows = packed[:, 2 * model_width : 3 * model_width]
    value_rows = packed[:, 3 * model_width :]
    head_count = model_width // HEAD_DIM
    key_heads = key_rows.reshape(tok_count, head_count, HEAD_DIM)
    value_heads = value_rows.reshape(tok_count, head_count, HEAD_DIM)
    seg_row = segment_ids[0]
    block_rows = min(tok_count, 512)
    block_count = tok_count // block_rows
    score_scale = 1.0 / math.sqrt(HEAD_DIM)

    def attend(block_args):
        query_block, seg_block = block_args
        query_heads = query_block.reshape(block_rows, head_count, HEAD_DIM)
        scores = (
            jnp.einsum("qhd,khd->hqk", query_heads, key_heads, preferred_element_type=jnp.float32)
            * score_scale
        )
        same_doc = seg_block[:, None] == seg_row[None, :]
        scores = jnp.where(same_doc[None, :, :], scores, mask_fill)
        top_score = jnp.max(scores, axis=2, keepdims=True)
        exp_terms = jnp.exp(scores - top_score)
        softmax_weights = (exp_terms / jnp.sum(exp_terms, axis=2, keepdims=True)).astype(
            jnp.bfloat16
        )
        mixed_heads = jnp.einsum(
            "hqk,khd->qhd", softmax_weights, value_heads, preferred_element_type=jnp.float32
        )
        return mixed_heads.reshape(block_rows, model_width)

    attended = lax.map(
        attend,
        (
            query_rows.reshape(block_count, block_rows, model_width),
            seg_row.reshape(block_count, block_rows),
        ),
    )
    hidden_state = state_rows.astype(jnp.float32) + attended.reshape(tok_count, model_width)
    mean_value = jnp.mean(hidden_state, axis=1, keepdims=True)
    centered = hidden_state - mean_value
    variance = jnp.mean(centered * centered, axis=1, keepdims=True)
    normed = (centered * lax.rsqrt(variance + epsilon) * ln_gain + ln_bias).astype(jnp.bfloat16)
    capacity = max(2, 2 * tok_count // (ROUNDS * expert_count))
    assigned = jnp.concatenate([expert_ids[:, 0], expert_ids[:, 1]])
    expert_hot = (assigned[:, None] == jnp.arange(expert_count, dtype=jnp.int32)[None, :]).astype(
        jnp.int32
    )
    slot_rank = jnp.sum(jnp.cumsum(expert_hot, axis=0) * expert_hot, axis=1) - 1
    kept_mask = (assigned < expert_count) & (slot_rank < capacity)
    overflow = expert_count * capacity
    slot_index = jnp.where(kept_mask, assigned * capacity + slot_rank, overflow)
    buffer = jnp.zeros((overflow, model_width), jnp.bfloat16)
    buffer = (
        buffer.at[slot_index[:tok_count]]
        .set(normed, mode="drop")
        .at[slot_index[tok_count:]]
        .set(normed, mode="drop")
    )
    arrived = lax.all_to_all(
        buffer.reshape(expert_count, capacity, model_width),
        "expert",
        split_axis=0,
        concat_axis=0,
        tiled=True,
    )
    arrived = arrived.reshape(overflow, model_width)
    results = experts(arrived, w_in, b_in, w_out, b_out)
    returned = lax.all_to_all(
        results.reshape(expert_count, capacity, model_width),
        "expert",
        split_axis=0,
        concat_axis=0,
        tiled=True,
    )
    returned = returned.reshape(overflow, model_width)
    gate_values = gate_code.astype(jnp.float32) / 65536.0
    gate_flat = jnp.concatenate([gate_values[:, 0], gate_values[:, 1]])
    weights = jnp.where(kept_mask, gate_flat, 0.0)
    guard_index = jnp.minimum(slot_index, overflow - 1)
    picked = returned[guard_index].astype(jnp.float32) * weights[:, None]
    layer_out = hidden_state + picked[:tok_count] + picked[tok_count:]
    return layer_out.astype(jnp.bfloat16)


def solution(mesh):
    return jax.shard_map(
        per_device,
        mesh=mesh,
        in_specs=(
            P(("dp", "expert"), None),
            P(("dp", "expert"), None),
            P(("dp", "expert"), None),
            P(("dp", "expert"), None),
            P(("dp", "expert")),
            P(("dp", "expert"), None),
            P(("dp", "expert"), None),
            P(("dp", "expert"), None),
            P(),
            P(),
            P("expert", None, "dp"),
            P("expert", "dp"),
            P("expert", "dp", None),
            P(),
        ),
        out_specs=P(("dp", "expert"), None),
        check_vma=False,
    )
```

```python
import math

import jax
import jax.numpy as jnp
from jax import lax
from jax.experimental import pallas as pl
from jax.experimental.pallas import tpu as pltpu
from jax.sharding import PartitionSpec as P

HEAD_DIM = 128
CAP = 2


epsilon = 1e-05
mask_fill = -1e30


MESH_ID = pl.DeviceIdType.MESH


def expert_kernel(
    x_ref,
    w1_ref,
    b1_ref,
    w2_ref,
    b2_ref,
    o_ref,
    rows,
    part,
    pair_in,
    run_out,
    run_in,
    w1_v,
    w2_v,
    load_sem,
    ag_send,
    ag_recv,
    sib_send,
    sib_recv,
    pair_send,
    pair_recv,
    run_send,
    run_recv,
):
    chips = lax.axis_size("dp") // 2
    me = lax.axis_index("dp")
    z = me // 2
    core = me % 2
    ahead = ((z + 1) % chips) * 2 + core
    behind = ((z + chips - 1) % chips) * 2 + core
    sibling = z * 2 + 1 - core
    half, width = rows.shape[3], rows.shape[4]
    steps = chips

    loads = (
        pltpu.make_async_copy(x_ref, rows.at[0, 0], load_sem.at[0]),
        pltpu.make_async_copy(w1_ref.at[0], w1_v, load_sem.at[1]),
        pltpu.make_async_copy(w2_ref.at[0], w2_v, load_sem.at[2]),
    )
    for load in loads:
        load.start()
    barrier = pltpu.get_barrier_semaphore()
    for peer in (ahead, behind, sibling):
        pl.semaphore_signal(barrier, inc=1, device_id={"dp": peer}, device_id_type=MESH_ID)
    pl.semaphore_wait(barrier, 3)
    loads[0].wait()

    def pass_on(s, way):
        return pltpu.make_async_remote_copy(
            src_ref=rows.at[s, 0, way],
            dst_ref=rows.at[s + 1, 0, way],
            send_sem=ag_send.at[s, way],
            recv_sem=ag_recv.at[s, way],
            device_id={"dp": (ahead, behind)[way]},
            device_id_type=MESH_ID,
        )

    def to_sibling(s):
        return pltpu.make_async_remote_copy(
            src_ref=rows.at[s, 0],
            dst_ref=rows.at[s, 1],
            send_sem=sib_send.at[s],
            recv_sem=sib_recv.at[s],
            device_id={"dp": sibling},
            device_id_type=MESH_ID,
        )

    def pair(s):
        return pltpu.make_async_remote_copy(
            src_ref=part.at[s, 1],
            dst_ref=pair_in.at[s],
            send_sem=pair_send.at[s],
            recv_sem=pair_recv.at[s],
            device_id={"dp": sibling},
            device_id_type=MESH_ID,
        )

    def run(s, way):
        return pltpu.make_async_remote_copy(
            src_ref=run_out.at[s - 1, way],
            dst_ref=run_in.at[s - 1, way],
            send_sem=run_send.at[s - 1, way],
            recv_sem=run_recv.at[s - 1, way],
            device_id={"dp": (ahead, behind)[way]},
            device_id_type=MESH_ID,
        )

    def step(i, carry):
        @pl.when(i < steps)
        def _():
            @pl.when(i >= 1)
            def _():
                for way in range(2):
                    pass_on(i - 1, way).wait_recv()

            @pl.when(i < steps - 1)
            def _():
                for way in range(2):
                    pass_on(i, way).start()

            to_sibling(i).start()

        @pl.when(i == 1)
        def _():
            loads[1].wait()
            loads[2].wait()

        @pl.when((i >= 1) & (i <= steps))
        def _():
            s = i - 1
            to_sibling(s).wait_recv()
            held = rows[s].reshape(4 * half, width)
            hidden = jnp.dot(held, w1_v[...], preferred_element_type=jnp.float32)
            hidden = jnp.maximum(hidden + b1_ref[...], 0.0).astype(jnp.bfloat16)
            share = jnp.dot(hidden, w2_v[...], preferred_element_type=jnp.float32)
            part[s] = share.astype(jnp.bfloat16).reshape(2, 2, half, width)
            pair(s).start()

        @pl.when(i == 3)
        def _():
            pair(1).wait_recv()
            total = part[1, 0].astype(jnp.float32) + pair_in[1].astype(jnp.float32)
            run_out[0] = total.astype(jnp.bfloat16)
            for way in range(2):
                run(1, way).start()

        @pl.when(i > 3)
        def _():
            s = i - 2
            pair(s).wait_recv()
            total = part[s, 0].astype(jnp.float32) + pair_in[s].astype(jnp.float32)
            for way in range(2):
                run(s - 1, way).wait_recv()
            total = total + run_in[s - 2].astype(jnp.float32)
            run_out[s - 1] = total.astype(jnp.bfloat16)
            for way in range(2):
                run(s, way).start()

        return carry

    lax.fori_loop(0, steps + 2, step, 0)
    pair(0).wait_recv()
    total = part[0, 0].astype(jnp.float32) + pair_in[0].astype(jnp.float32)
    total = total + b2_ref[pl.ds(lax.axis_index("expert"), 1), :].reshape(1, 1, width)
    for way in range(2):
        run(steps - 1, way).wait_recv()
    total = total + run_in[steps - 2].astype(jnp.float32)
    o_ref[...] = total.astype(jnp.bfloat16).reshape(2 * half, width)

    def drain(s, carry):
        to_sibling(s).wait_send()
        pair(s).wait_send()

        @pl.when(s < steps - 1)
        def _():
            for way in range(2):
                pass_on(s, way).wait_send()
                run(s + 1, way).wait_send()

        return carry

    lax.fori_loop(0, steps, drain, 0)


def experts(arrived, w_in, b_in, w_out, b_out):
    count, width = arrived.shape
    units = w_in.shape[2]
    half = count // 2
    chips = lax.axis_size("dp") // 2
    dma = pltpu.SemaphoreType.DMA
    bf16 = jnp.bfloat16
    any_space = pl.BlockSpec(memory_space=pl.ANY)
    vmem = pl.BlockSpec(memory_space=pltpu.VMEM)
    return pl.pallas_call(
        expert_kernel,
        out_shape=jax.ShapeDtypeStruct((count, width), bf16),
        in_specs=[any_space, any_space, vmem, any_space, vmem],
        out_specs=vmem,
        scratch_shapes=[
            pltpu.VMEM((chips, 2, 2, half, width), bf16),
            pltpu.VMEM((chips, 2, 2, half, width), bf16),
            pltpu.VMEM((chips, 2, half, width), bf16),
            pltpu.VMEM((chips - 1, 2, half, width), bf16),
            pltpu.VMEM((chips - 1, 2, half, width), bf16),
            pltpu.VMEM((width, units), bf16),
            pltpu.VMEM((units, width), bf16),
            dma((3,)),
            dma((chips - 1, 2)),
            dma((chips - 1, 2)),
            dma((chips,)),
            dma((chips,)),
            dma((chips,)),
            dma((chips,)),
            dma((chips - 1, 2)),
            dma((chips - 1, 2)),
        ],
        compiler_params=pltpu.CompilerParams(collective_id=1, has_side_effects=True),
        name="expert_ring",
    )(arrived.reshape(2, half, width), w_in, b_in, w_out, b_out)


F32 = jnp.float32
BF16 = jnp.bfloat16


def iota(shape, axis):
    return lax.broadcasted_iota(jnp.int32, shape, axis)


def as_column(row):
    count = row.shape[1]
    return jnp.transpose(jnp.broadcast_to(row, (count, count)))


def earlier_equal(row):
    count = row.shape[1]
    same = as_column(row) == jnp.broadcast_to(row, (count, count))
    before = iota((count, count), 0) < iota((count, count), 1)
    return jnp.sum((same & before).astype(F32), axis=0, keepdims=True)


def slot_row(ids_ref, expert_count):
    ids = ids_ref[...].astype(F32)
    assigned = jnp.concatenate([ids[0:1, :], ids[1:2, :]], axis=1)
    rank = earlier_equal(assigned)
    kept = (assigned < expert_count) & (rank < CAP)
    return jnp.where(kept, assigned * CAP + rank, -1.0)


def regroup_kernel(
    pos_ref,
    seg_ref,
    ids_ref,
    gain_ref,
    bias_ref,
    state_ref,
    query_ref,
    key_ref,
    value_ref,
    hidden_ref,
    buffer_ref,
    out_rows,
    in_rows,
    out_offs,
    in_offs,
    send_sem,
    recv_sem,
):
    peers = lax.axis_size("dp")
    experts_here = lax.axis_size("expert")
    me = lax.axis_index("dp")
    tokens, width = state_ref.shape
    per_target = tokens // peers
    chunks = out_rows.shape[0]
    part = width // chunks
    both = 2 * tokens

    barrier = pltpu.get_barrier_semaphore()

    def greet(k, carry):
        pl.semaphore_signal(
            barrier, inc=1, device_id={"dp": (me + k) % peers}, device_id_type=MESH_ID
        )
        return carry

    lax.fori_loop(1, peers, greet, 0)

    pos = pos_ref[...]
    target = (pos // tokens).astype(F32)
    offset = (pos % tokens).astype(F32)
    place = target * (2 * per_target) + earlier_equal(target)
    places = jnp.concatenate([place, place + per_target], axis=1).astype(jnp.int32)
    spread = (iota((both, both), 0) == places).astype(F32).astype(BF16)
    offset_column = as_column(offset)
    offset_both = jnp.concatenate([offset_column, offset_column + tokens], axis=0).astype(BF16)
    out_offs[...] = (
        jnp.dot(spread, offset_both, preferred_element_type=F32)
        .astype(BF16)
        .reshape(peers, 2 * per_target, tokens)
    )

    def fill(c):
        cols = pl.ds(pl.multiple_of(c * part, part), part)
        upper = jnp.concatenate([state_ref[:, cols], query_ref[:, cols]], axis=1)
        lower = jnp.concatenate([key_ref[:, cols], value_ref[:, cols]], axis=1)
        joined = jnp.concatenate([upper, lower], axis=0)
        out_rows[c] = (
            jnp.dot(spread, joined, preferred_element_type=F32)
            .astype(BF16)
            .reshape(peers, 2 * per_target, 2 * part)
        )

    def send_rows(c, to, frm):
        return pltpu.make_async_remote_copy(
            src_ref=out_rows.at[c, to],
            dst_ref=in_rows.at[c, frm],
            send_sem=send_sem.at[c, to],
            recv_sem=recv_sem.at[c, frm],
            device_id={"dp": to},
            device_id_type=MESH_ID,
        )

    def send_offs(to, frm):
        return pltpu.make_async_remote_copy(
            src_ref=out_offs.at[to],
            dst_ref=in_offs.at[frm],
            send_sem=send_sem.at[chunks, to],
            recv_sem=recv_sem.at[chunks, frm],
            device_id={"dp": to},
            device_id_type=MESH_ID,
        )

    def own_rows(c):
        return pltpu.make_async_copy(out_rows.at[c, me], in_rows.at[c, me], recv_sem.at[c, me])

    own_offs = pltpu.make_async_copy(out_offs.at[me], in_offs.at[me], recv_sem.at[chunks, me])

    def order(k):
        step = (k + 1) // 2
        return (me + peers + step * (2 * (k % 2) - 1)) % peers

    fill(0)
    pl.semaphore_wait(barrier, peers - 1)
    own_offs.start()

    def start_offs(k, carry):
        send_offs(order(k), me).start()
        return carry

    lax.fori_loop(1, peers, start_offs, 0)

    def start_chunk(c, carry):
        @pl.when(c > 0)
        def _():
            fill(c)

        own_rows(c).start()

        def start_rows(k, inner):
            send_rows(c, order(k), me).start()
            return inner

        return lax.fori_loop(1, peers, start_rows, carry)

    lax.fori_loop(0, chunks, start_chunk, 0)

    slots = slot_row(ids_ref, experts_here)
    slot_hot = (iota((experts_here * CAP, both), 0) == slots.astype(jnp.int32)).astype(F32)
    slot_hot = (slot_hot[:, :tokens] + slot_hot[:, tokens:]).astype(BF16)
    segs = seg_ref[...].astype(F32)
    same_doc = as_column(segs) == jnp.broadcast_to(segs, (tokens, tokens))

    own_offs.wait()

    def await_offs(k, carry):
        send_offs(me, (me + k) % peers).wait_recv()
        return carry

    lax.fori_loop(1, peers, await_offs, 0)
    offs = in_offs[...].reshape(both, tokens).astype(F32)
    lanes = iota((both, tokens), 1).astype(F32)
    gather = jnp.concatenate([offs == lanes, offs == lanes + tokens], axis=1).astype(F32)
    gather = jnp.transpose(gather).astype(BF16)
    score_scale = 1.0 / math.sqrt(HEAD_DIM)

    def attend(c, carry):
        own_rows(c).wait()

        def await_rows(k, inner):
            send_rows(c, me, (me + k) % peers).wait_recv()
            return inner

        lax.fori_loop(1, peers, await_rows, 0)
        packed = jnp.dot(
            gather, in_rows[c].reshape(both, 2 * part), preferred_element_type=F32
        )
        states = packed[:tokens, :part]
        query = packed[:tokens, part:].astype(BF16)
        key = packed[tokens:, :part].astype(BF16)
        value = packed[tokens:, part:].astype(BF16)
        for h in range(part // HEAD_DIM):
            cols = slice(h * HEAD_DIM, (h + 1) * HEAD_DIM)
            scores = lax.dot_general(
                query[:, cols],
                key[:, cols],
                (((1,), (1,)), ((), ())),
                preferred_element_type=F32,
            )
            scores = jnp.where(same_doc, scores * score_scale, mask_fill)
            terms = jnp.exp(scores - jnp.max(scores, axis=1, keepdims=True))
            probs = (terms / jnp.sum(terms, axis=1, keepdims=True)).astype(BF16)
            mixed = jnp.dot(probs, value[:, cols], preferred_element_type=F32)
            at = pl.ds(pl.multiple_of(c * part + h * HEAD_DIM, HEAD_DIM), HEAD_DIM)
            hidden_ref[:, at] = states[:, cols] + mixed
        return carry

    lax.fori_loop(0, chunks, attend, 0)
    hidden = hidden_ref[...]
    centered = hidden - jnp.mean(hidden, axis=1, keepdims=True)
    variance = jnp.mean(centered * centered, axis=1, keepdims=True)
    normed = centered * lax.rsqrt(variance + epsilon) * gain_ref[...] + bias_ref[...]
    buffer_ref[...] = jnp.dot(
        slot_hot, normed.astype(BF16), preferred_element_type=F32
    ).astype(BF16)

    def drain(k, carry):
        peer = (me + k) % peers
        send_offs(peer, me).wait_send()

        def drain_chunk(c, inner):
            send_rows(c, peer, me).wait_send()
            return inner

        return lax.fori_loop(0, chunks, drain_chunk, carry)

    lax.fori_loop(1, peers, drain, 0)


def regroup_attend(states, queries, keys, values, pos, segs, ids, gain, bias):
    tokens, width = states.shape
    peers = lax.axis_size("dp")
    slots = lax.axis_size("expert") * CAP
    chunks = 4
    group = 2 * tokens // peers
    dma = pltpu.SemaphoreType.DMA
    vmem = pl.BlockSpec(memory_space=pltpu.VMEM)
    return pl.pallas_call(
        regroup_kernel,
        out_shape=(
            jax.ShapeDtypeStruct((tokens, width), F32),
            jax.ShapeDtypeStruct((slots, width), BF16),
        ),
        in_specs=[vmem] * 9,
        out_specs=(vmem, vmem),
        scratch_shapes=[
            pltpu.VMEM((chunks, peers, group, 2 * width // chunks), BF16),
            pltpu.VMEM((chunks, peers, group, 2 * width // chunks), BF16),
            pltpu.VMEM((peers, group, tokens), BF16),
            pltpu.VMEM((peers, group, tokens), BF16),
            dma((chunks + 1, peers)),
            dma((chunks + 1, peers)),
        ],
        compiler_params=pltpu.CompilerParams(collective_id=2, has_side_effects=True),
        name="regroup_attend",
    )(pos, segs, ids, gain, bias, states, queries, keys, values)


def exchange_kernel(x_ref, o_ref, send_sem, recv_sem):
    peers = lax.axis_size("expert")
    me = lax.axis_index("expert")
    barrier = pltpu.get_barrier_semaphore()

    def greet(k, carry):
        pl.semaphore_signal(
            barrier, inc=1, device_id={"expert": (me + k) % peers}, device_id_type=MESH_ID
        )
        return carry

    lax.fori_loop(1, peers, greet, 0)
    own = pltpu.make_async_copy(x_ref.at[me], o_ref.at[me], recv_sem.at[me])
    own.start()
    pl.semaphore_wait(barrier, peers - 1)

    def move(to, frm):
        return pltpu.make_async_remote_copy(
            src_ref=x_ref.at[to],
            dst_ref=o_ref.at[frm],
            send_sem=send_sem.at[to],
            recv_sem=recv_sem.at[frm],
            device_id={"expert": to},
            device_id_type=MESH_ID,
        )

    def start(k, carry):
        move((me + k) % peers, me).start()
        return carry

    lax.fori_loop(1, peers, start, 0)
    own.wait()

    def finish(k, carry):
        peer = (me + k) % peers
        move(me, peer).wait_recv()
        move(peer, me).wait_send()
        return carry

    lax.fori_loop(1, peers, finish, 0)


def exchange(rows, call_id):
    peers = lax.axis_size("expert")
    count, width = rows.shape
    shape = (peers, count // peers, width)
    dma = pltpu.SemaphoreType.DMA
    vmem = pl.BlockSpec(memory_space=pltpu.VMEM)
    moved = pl.pallas_call(
        exchange_kernel,
        out_shape=jax.ShapeDtypeStruct(shape, rows.dtype),
        in_specs=[vmem],
        out_specs=vmem,
        scratch_shapes=[dma((peers,)), dma((peers,))],
        compiler_params=pltpu.CompilerParams(collective_id=call_id, has_side_effects=True),
        name="exchange",
    )(rows.reshape(shape))
    return moved.reshape(count, width)


def combine_kernel(hidden_ref, ids_ref, gate_ref, rows_ref, o_ref):
    tokens = hidden_ref.shape[0]
    count = rows_ref.shape[0]
    slots = slot_row(ids_ref, count // CAP)
    total = hidden_ref[...]
    gates = gate_ref[...].astype(F32) / 65536.0
    for choice in range(2):
        column = as_column(slots[:, choice * tokens : (choice + 1) * tokens])
        hot = (column == iota((tokens, tokens), 1).astype(F32)).astype(F32).astype(BF16)
        picked = jnp.dot(hot[:, :count], rows_ref[...], preferred_element_type=F32)
        total = total + picked * gates[:, choice : choice + 1]
    o_ref[...] = total.astype(BF16)


def combine(hidden, ids, gate_code, rows):
    vmem = pl.BlockSpec(memory_space=pltpu.VMEM)
    return pl.pallas_call(
        combine_kernel,
        out_shape=jax.ShapeDtypeStruct(hidden.shape, BF16),
        in_specs=[vmem] * 4,
        out_specs=vmem,
        name="combine",
    )(hidden, ids, gate_code, rows)


def per_device(
    pivot_states,
    queries,
    keys,
    values,
    pack_pos,
    segment_ids,
    expert_ids,
    gate_code,
    ln_gain,
    ln_bias,
    w_in,
    b_in,
    w_out,
    b_out,
):
    ids = expert_ids.T
    hidden_state, buffer = regroup_attend(
        pivot_states,
        queries,
        keys,
        values,
        pack_pos[None, :],
        segment_ids,
        ids,
        ln_gain[None, :],
        ln_bias[None, :],
    )
    arrived = exchange(buffer, 3)
    results = experts(arrived, w_in, b_in, w_out, b_out)
    returned = exchange(results, 4)
    return combine(hidden_state, ids, gate_code, returned)


def solution(mesh):
    return jax.shard_map(
        per_device,
        mesh=mesh,
        in_specs=(
            P(("dp", "expert"), None),
            P(("dp", "expert"), None),
            P(("dp", "expert"), None),
            P(("dp", "expert"), None),
            P(("dp", "expert")),
            P(("dp", "expert"), None),
            P(("dp", "expert"), None),
            P(("dp", "expert"), None),
            P(),
            P(),
            P("expert", None, "dp"),
            P("expert", "dp"),
            P("expert", "dp", None),
            P(),
        ),
        out_specs=P(("dp", "expert"), None),
        check_vma=False,
    )
```

```python
import math

import jax
import jax.numpy as jnp
from jax import lax
from jax.experimental import pallas as pl
from jax.experimental.pallas import tpu as pltpu
from jax.sharding import PartitionSpec as P

HEAD_DIM = 128
CAP = 2


epsilon = 1e-05
mask_fill = -1e30


MESH_ID = pl.DeviceIdType.MESH


F32 = jnp.float32
BF16 = jnp.bfloat16


def iota(shape, axis):
    return lax.broadcasted_iota(jnp.int32, shape, axis)


def as_column(row):
    count = row.shape[1]
    return jnp.transpose(jnp.broadcast_to(row, (count, count)))


def earlier_equal(row):
    count = row.shape[1]
    same = as_column(row) == jnp.broadcast_to(row, (count, count))
    before = iota((count, count), 0) < iota((count, count), 1)
    return jnp.sum((same & before).astype(F32), axis=0, keepdims=True)


def slot_row(ids_ref, expert_count):
    ids = ids_ref[...].astype(F32)
    assigned = jnp.concatenate([ids[0:1, :], ids[1:2, :]], axis=1)
    rank = earlier_equal(assigned)
    kept = (assigned < expert_count) & (rank < CAP)
    return jnp.where(kept, assigned * CAP + rank, -1.0)


def regroup_phase(
    pos_ref,
    seg_ref,
    gain_ref,
    bias_ref,
    state_ref,
    query_ref,
    key_ref,
    value_ref,
    hidden_ref,
    out_rows,
    in_rows,
    out_offs,
    in_offs,
    send_sem,
    recv_sem,
    await_barrier,
):
    peers = lax.axis_size("dp")
    me = lax.axis_index("dp")
    tokens, width = state_ref.shape
    per_target = tokens // peers
    chunks = out_rows.shape[0]
    part = width // chunks
    both = 2 * tokens

    pos = pos_ref[...]
    target = (pos // tokens).astype(F32)
    offset = (pos % tokens).astype(F32)
    place = target * (2 * per_target) + earlier_equal(target)
    places = jnp.concatenate([place, place + per_target], axis=1).astype(jnp.int32)
    spread = (iota((both, both), 0) == places).astype(F32).astype(BF16)
    offset_column = as_column(offset)
    offset_both = jnp.concatenate([offset_column, offset_column + tokens], axis=0).astype(BF16)
    out_offs[...] = (
        jnp.dot(spread, offset_both, preferred_element_type=F32)
        .astype(BF16)
        .reshape(peers, 2 * per_target, tokens)
    )

    def fill(c):
        cols = pl.ds(pl.multiple_of(c * part, part), part)
        upper = jnp.concatenate([state_ref[:, cols], query_ref[:, cols]], axis=1)
        lower = jnp.concatenate([key_ref[:, cols], value_ref[:, cols]], axis=1)
        joined = jnp.concatenate([upper, lower], axis=0)
        out_rows[c] = (
            jnp.dot(spread, joined, preferred_element_type=F32)
            .astype(BF16)
            .reshape(peers, 2 * per_target, 2 * part)
        )

    def send_rows(c, to, frm):
        return pltpu.make_async_remote_copy(
            src_ref=out_rows.at[c, to],
            dst_ref=in_rows.at[c, frm],
            send_sem=send_sem.at[c, to],
            recv_sem=recv_sem.at[c, frm],
            device_id={"dp": to},
            device_id_type=MESH_ID,
        )

    def send_offs(to, frm):
        return pltpu.make_async_remote_copy(
            src_ref=out_offs.at[to],
            dst_ref=in_offs.at[frm],
            send_sem=send_sem.at[chunks, to],
            recv_sem=recv_sem.at[chunks, frm],
            device_id={"dp": to},
            device_id_type=MESH_ID,
        )

    def own_rows(c):
        return pltpu.make_async_copy(out_rows.at[c, me], in_rows.at[c, me], recv_sem.at[c, me])

    own_offs = pltpu.make_async_copy(out_offs.at[me], in_offs.at[me], recv_sem.at[chunks, me])

    def order(k):
        step = (k + 1) // 2
        return (me + peers + step * (2 * (k % 2) - 1)) % peers

    fill(0)
    await_barrier()
    own_offs.start()

    def start_offs(k, carry):
        send_offs(order(k), me).start()
        return carry

    lax.fori_loop(1, peers, start_offs, 0)

    def start_chunk(c, carry):
        @pl.when(c > 0)
        def _():
            fill(c)

        own_rows(c).start()

        def start_rows(k, inner):
            send_rows(c, order(k), me).start()
            return inner

        return lax.fori_loop(1, peers, start_rows, carry)

    lax.fori_loop(0, chunks, start_chunk, 0)

    segs = seg_ref[...].astype(F32)
    same_doc = as_column(segs) == jnp.broadcast_to(segs, (tokens, tokens))

    own_offs.wait()

    def await_offs(k, carry):
        send_offs(me, (me + k) % peers).wait_recv()
        return carry

    lax.fori_loop(1, peers, await_offs, 0)
    offs = in_offs[...].reshape(both, tokens).astype(F32)
    lanes = iota((both, tokens), 1).astype(F32)
    gather = jnp.concatenate([offs == lanes, offs == lanes + tokens], axis=1).astype(F32)
    gather = jnp.transpose(gather).astype(BF16)
    score_scale = 1.0 / math.sqrt(HEAD_DIM)

    def attend(c, carry):
        own_rows(c).wait()

        def await_rows(k, inner):
            send_rows(c, me, (me + k) % peers).wait_recv()
            return inner

        lax.fori_loop(1, peers, await_rows, 0)
        packed = jnp.dot(
            gather, in_rows[c].reshape(both, 2 * part), preferred_element_type=F32
        )
        states = packed[:tokens, :part]
        query = packed[:tokens, part:].astype(BF16)
        key = packed[tokens:, :part].astype(BF16)
        value = packed[tokens:, part:].astype(BF16)
        for h in range(part // HEAD_DIM):
            cols = slice(h * HEAD_DIM, (h + 1) * HEAD_DIM)
            scores = lax.dot_general(
                query[:, cols],
                key[:, cols],
                (((1,), (1,)), ((), ())),
                preferred_element_type=F32,
            )
            scores = jnp.where(same_doc, scores * score_scale, mask_fill)
            terms = jnp.exp(scores - jnp.max(scores, axis=1, keepdims=True))
            probs = (terms / jnp.sum(terms, axis=1, keepdims=True)).astype(BF16)
            mixed = jnp.dot(probs, value[:, cols], preferred_element_type=F32)
            at = pl.ds(pl.multiple_of(c * part + h * HEAD_DIM, HEAD_DIM), HEAD_DIM)
            hidden_ref[:, at] = states[:, cols] + mixed
        return carry

    lax.fori_loop(0, chunks, attend, 0)
    hidden = hidden_ref[...]
    centered = hidden - jnp.mean(hidden, axis=1, keepdims=True)
    variance = jnp.mean(centered * centered, axis=1, keepdims=True)
    normed = centered * lax.rsqrt(variance + epsilon) * gain_ref[...] + bias_ref[...]
    def drain(k, carry):
        peer = (me + k) % peers
        send_offs(peer, me).wait_send()

        def drain_chunk(c, inner):
            send_rows(c, peer, me).wait_send()
            return inner

        return lax.fori_loop(0, chunks, drain_chunk, carry)

    return normed.astype(BF16), lambda: lax.fori_loop(1, peers, drain, 0)


def expert_phase(
    b1_ref,
    b2_ref,
    loads,
    rows,
    part,
    pair_in,
    run_out,
    run_in,
    w1_v,
    w2_v,
    ag_send,
    ag_recv,
    sib_send,
    sib_recv,
    pair_send,
    pair_recv,
    run_send,
    run_recv,
):
    chips = lax.axis_size("dp") // 2
    me = lax.axis_index("dp")
    z = me // 2
    core = me % 2
    ahead = ((z + 1) % chips) * 2 + core
    behind = ((z + chips - 1) % chips) * 2 + core
    sibling = z * 2 + 1 - core
    half, width = rows.shape[3], rows.shape[4]
    steps = chips

    def pass_on(s, way):
        return pltpu.make_async_remote_copy(
            src_ref=rows.at[s, 0, way],
            dst_ref=rows.at[s + 1, 0, way],
            send_sem=ag_send.at[s, way],
            recv_sem=ag_recv.at[s, way],
            device_id={"dp": (ahead, behind)[way]},
            device_id_type=MESH_ID,
        )

    def to_sibling(s):
        return pltpu.make_async_remote_copy(
            src_ref=rows.at[s, 0],
            dst_ref=rows.at[s, 1],
            send_sem=sib_send.at[s],
            recv_sem=sib_recv.at[s],
            device_id={"dp": sibling},
            device_id_type=MESH_ID,
        )

    def pair(s):
        return pltpu.make_async_remote_copy(
            src_ref=part.at[s, 1],
            dst_ref=pair_in.at[s],
            send_sem=pair_send.at[s],
            recv_sem=pair_recv.at[s],
            device_id={"dp": sibling},
            device_id_type=MESH_ID,
        )

    def run(s, way):
        return pltpu.make_async_remote_copy(
            src_ref=run_out.at[s - 1, way],
            dst_ref=run_in.at[s - 1, way],
            send_sem=run_send.at[s - 1, way],
            recv_sem=run_recv.at[s - 1, way],
            device_id={"dp": (ahead, behind)[way]},
            device_id_type=MESH_ID,
        )

    def step(i, carry):
        @pl.when(i < steps)
        def _():
            @pl.when(i >= 1)
            def _():
                for way in range(2):
                    pass_on(i - 1, way).wait_recv()

            @pl.when(i < steps - 1)
            def _():
                for way in range(2):
                    pass_on(i, way).start()

            to_sibling(i).start()

        @pl.when(i == 1)
        def _():
            for load in loads:
                load.wait()

        @pl.when((i >= 1) & (i <= steps))
        def _():
            s = i - 1
            to_sibling(s).wait_recv()
            held = rows[s].reshape(4 * half, width)
            hidden = jnp.dot(held, w1_v[...], preferred_element_type=jnp.float32)
            hidden = jnp.maximum(hidden + b1_ref[...], 0.0).astype(jnp.bfloat16)
            share = jnp.dot(hidden, w2_v[...], preferred_element_type=jnp.float32)
            part[s] = share.astype(jnp.bfloat16).reshape(2, 2, half, width)
            pair(s).start()

        @pl.when(i == 3)
        def _():
            pair(1).wait_recv()
            total = part[1, 0].astype(jnp.float32) + pair_in[1].astype(jnp.float32)
            run_out[0] = total.astype(jnp.bfloat16)
            for way in range(2):
                run(1, way).start()

        @pl.when(i > 3)
        def _():
            s = i - 2
            pair(s).wait_recv()
            total = part[s, 0].astype(jnp.float32) + pair_in[s].astype(jnp.float32)
            for way in range(2):
                run(s - 1, way).wait_recv()
            total = total + run_in[s - 2].astype(jnp.float32)
            run_out[s - 1] = total.astype(jnp.bfloat16)
            for way in range(2):
                run(s, way).start()

        return carry

    lax.fori_loop(0, steps + 2, step, 0)
    pair(0).wait_recv()
    total = part[0, 0].astype(jnp.float32) + pair_in[0].astype(jnp.float32)
    total = total + b2_ref[pl.ds(lax.axis_index("expert"), 1), :].reshape(1, 1, width)
    for way in range(2):
        run(steps - 1, way).wait_recv()
    total = total + run_in[steps - 2].astype(jnp.float32)
    results = total.reshape(2 * half, width)

    def drain(s, carry):
        to_sibling(s).wait_send()
        pair(s).wait_send()

        @pl.when(s < steps - 1)
        def _():
            for way in range(2):
                pass_on(s, way).wait_send()
                run(s + 1, way).wait_send()

        return carry

    return results, lambda: lax.fori_loop(0, steps, drain, 0)


def exchange_phase(out_ref, in_ref, send_sem, recv_sem):
    peers = lax.axis_size("expert")
    me = lax.axis_index("expert")
    own = pltpu.make_async_copy(out_ref.at[me], in_ref.at[me], recv_sem.at[me])

    def move(to, frm):
        return pltpu.make_async_remote_copy(
            src_ref=out_ref.at[to],
            dst_ref=in_ref.at[frm],
            send_sem=send_sem.at[to],
            recv_sem=recv_sem.at[frm],
            device_id={"expert": to},
            device_id_type=MESH_ID,
        )

    def start(k, carry):
        move((me + k) % peers, me).start()
        return carry

    lax.fori_loop(1, peers, start, 0)
    own.start()
    own.wait()

    def finish(k, carry):
        move(me, (me + k) % peers).wait_recv()
        return carry

    lax.fori_loop(1, peers, finish, 0)

    def drain(k, carry):
        move((me + k) % peers, me).wait_send()
        return carry

    return lambda: lax.fori_loop(1, peers, drain, 0)


def layer_kernel(
    pos_ref,
    seg_ref,
    ids_ref,
    gate_ref,
    gain_ref,
    bias_ref,
    state_ref,
    query_ref,
    key_ref,
    value_ref,
    w1_ref,
    b1_ref,
    w2_ref,
    b2_ref,
    o_ref,
    hidden_ref,
    out_rows,
    in_rows,
    out_offs,
    in_offs,
    send_sem,
    recv_sem,
    stage,
    out_msgs,
    in_msgs,
    back_out,
    back_in,
    msg_send,
    msg_recv,
    load_sem,
    rows,
    part,
    pair_in,
    run_out,
    run_in,
    w1_v,
    w2_v,
    *ring_sems,
):
    dp_count = lax.axis_size("dp")
    expert_count = lax.axis_size("expert")
    dp_me = lax.axis_index("dp")
    expert_me = lax.axis_index("expert")
    tokens, width = state_ref.shape
    count = expert_count * CAP
    piece = stage.shape[2]
    pieces = stage.shape[1]
    loads = (
        pltpu.make_async_copy(w1_ref.at[0], w1_v, load_sem.at[0]),
        pltpu.make_async_copy(w2_ref.at[0], w2_v, load_sem.at[1]),
    )
    barrier = pltpu.get_barrier_semaphore()

    def greet_expert(k, carry):
        peer = (expert_me + k) % expert_count
        pl.semaphore_signal(barrier, inc=1, device_id={"expert": peer}, device_id_type=MESH_ID)
        return carry

    def greet_dp(k, carry):
        peer = (dp_me + k) % dp_count
        pl.semaphore_signal(barrier, inc=1, device_id={"dp": peer}, device_id_type=MESH_ID)
        return carry

    lax.fori_loop(1, expert_count, greet_expert, 0)
    lax.fori_loop(1, dp_count, greet_dp, 0)
    for load in loads:
        load.start()

    normed, drain_rows = regroup_phase(
        pos_ref,
        seg_ref,
        gain_ref,
        bias_ref,
        state_ref,
        query_ref,
        key_ref,
        value_ref,
        hidden_ref,
        out_rows,
        in_rows,
        out_offs,
        in_offs,
        send_sem,
        recv_sem,
        lambda: pl.semaphore_wait(barrier, dp_count + expert_count - 2),
    )

    def pack(ref):
        ref[...] = stage[...].reshape(ref.shape[0] * ref.shape[1], piece).astype(BF16).reshape(ref.shape)

    def unpack(ref):
        stage[...] = ref[...].reshape(ref.shape[0] * ref.shape[1], piece).astype(F32).reshape(stage.shape)

    slots = slot_row(ids_ref, expert_count)
    slot_hot = (iota((count, 2 * tokens), 0) == slots.astype(jnp.int32)).astype(F32)
    slot_hot = (slot_hot[:, :tokens] + slot_hot[:, tokens:]).astype(BF16)
    buffer = jnp.dot(slot_hot, normed, preferred_element_type=F32)
    for b in range(pieces):
        stage[:, b, :] = buffer[:, b * piece : (b + 1) * piece]
    pack(out_msgs)
    drain_out = exchange_phase(out_msgs, in_msgs, msg_send.at[0], msg_recv.at[0])
    unpack(in_msgs)
    half = count // 2
    for b in range(pieces):
        rows[0, 0, :, :, b * piece : (b + 1) * piece] = (
            stage[:, b, :].astype(BF16).reshape(2, half, piece)
        )
    results, drain_ring = expert_phase(
        b1_ref, b2_ref, loads, rows, part, pair_in, run_out, run_in, w1_v, w2_v, *ring_sems
    )
    for b in range(pieces):
        stage[:, b, :] = results[:, b * piece : (b + 1) * piece]
    pack(back_out)
    drain_back = exchange_phase(back_out, back_in, msg_send.at[1], msg_recv.at[1])
    unpack(back_in)

    gates = gate_ref[...].astype(F32) / 65536.0
    hots, weights = [], []
    for choice in range(2):
        column = as_column(slots[:, choice * tokens : (choice + 1) * tokens])
        hot = (column == iota((tokens, tokens), 1).astype(F32)).astype(F32).astype(BF16)
        hots.append(hot[:, :count])
        weights.append(as_column(gates[choice : choice + 1, :])[:, 0:1])
    for b in range(pieces):
        cols = slice(b * piece, (b + 1) * piece)
        returned = stage[:, b, :].astype(BF16)
        total = hidden_ref[:, cols]
        for hot, weight in zip(hots, weights):
            total = total + jnp.dot(hot, returned, preferred_element_type=F32) * weight
        o_ref[:, cols] = total.astype(BF16)
    drain_rows()
    drain_out()
    drain_ring()
    drain_back()


def per_device(
    pivot_states,
    queries,
    keys,
    values,
    pack_pos,
    segment_ids,
    expert_ids,
    gate_code,
    ln_gain,
    ln_bias,
    w_in,
    b_in,
    w_out,
    b_out,
):
    tokens, width = pivot_states.shape
    units = w_in.shape[2]
    peers = lax.axis_size("dp")
    expert_count = lax.axis_size("expert")
    count = expert_count * CAP
    half = count // 2
    chips = peers // 2
    chunks = 4
    group = 2 * tokens // peers
    pieces = 8
    piece = width // pieces
    dma = pltpu.SemaphoreType.DMA
    vmem = pl.BlockSpec(memory_space=pltpu.VMEM)
    any_space = pl.BlockSpec(memory_space=pl.ANY)
    messages = pltpu.VMEM((expert_count, CAP * pieces, piece), BF16)
    return pl.pallas_call(
        layer_kernel,
        out_shape=jax.ShapeDtypeStruct((tokens, width), BF16),
        in_specs=[vmem] * 10 + [any_space, vmem, any_space, vmem],
        out_specs=vmem,
        scratch_shapes=[
            pltpu.VMEM((tokens, width), F32),
            pltpu.VMEM((chunks, peers, group, 2 * width // chunks), BF16),
            pltpu.VMEM((chunks, peers, group, 2 * width // chunks), BF16),
            pltpu.VMEM((peers, group, tokens), BF16),
            pltpu.VMEM((peers, group, tokens), BF16),
            dma((chunks + 1, peers)),
            dma((chunks + 1, peers)),
            pltpu.VMEM((count, pieces, piece), F32),
            messages,
            messages,
            messages,
            messages,
            dma((2, expert_count)),
            dma((2, expert_count)),
            dma((2,)),
            pltpu.VMEM((chips, 2, 2, half, width), BF16),
            pltpu.VMEM((chips, 2, 2, half, width), BF16),
            pltpu.VMEM((chips, 2, half, width), BF16),
            pltpu.VMEM((chips - 1, 2, half, width), BF16),
            pltpu.VMEM((chips - 1, 2, half, width), BF16),
            pltpu.VMEM((width, units), BF16),
            pltpu.VMEM((units, width), BF16),
            dma((chips - 1, 2)),
            dma((chips - 1, 2)),
            dma((chips,)),
            dma((chips,)),
            dma((chips,)),
            dma((chips,)),
            dma((chips - 1, 2)),
            dma((chips - 1, 2)),
        ],
        compiler_params=pltpu.CompilerParams(collective_id=1, has_side_effects=True),
        name="moe_layer",
    )(
        pack_pos[None, :],
        segment_ids,
        expert_ids.T,
        gate_code.T,
        ln_gain[None, :],
        ln_bias[None, :],
        pivot_states,
        queries,
        keys,
        values,
        w_in,
        b_in,
        w_out,
        b_out,
    )


def solution(mesh):
    return jax.shard_map(
        per_device,
        mesh=mesh,
        in_specs=(
            P(("dp", "expert"), None),
            P(("dp", "expert"), None),
            P(("dp", "expert"), None),
            P(("dp", "expert"), None),
            P(("dp", "expert")),
            P(("dp", "expert"), None),
            P(("dp", "expert"), None),
            P(("dp", "expert"), None),
            P(),
            P(),
            P("expert", None, "dp"),
            P("expert", "dp"),
            P("expert", "dp", None),
            P(),
        ),
        out_specs=P(("dp", "expert"), None),
        check_vma=False,
    )
```

```python
import math

import jax
import jax.numpy as jnp
from jax import lax
from jax.experimental import pallas as pl
from jax.experimental.pallas import tpu as pltpu
from jax.sharding import PartitionSpec as P

HEAD_DIM = 128
CAP = 2


epsilon = 1e-05
mask_fill = -1e30


MESH_ID = pl.DeviceIdType.MESH


F32 = jnp.float32
BF16 = jnp.bfloat16


def iota(shape, axis):
    return lax.broadcasted_iota(jnp.int32, shape, axis)


def as_column(row):
    count = row.shape[1]
    return jnp.transpose(jnp.broadcast_to(row, (count, count)))


def earlier_equal(row):
    count = row.shape[1]
    same = as_column(row) == jnp.broadcast_to(row, (count, count))
    before = iota((count, count), 0) < iota((count, count), 1)
    return jnp.sum((same & before).astype(F32), axis=0, keepdims=True)


def slot_row(ids_ref, expert_count):
    ids = ids_ref[...].astype(F32)
    assigned = jnp.concatenate([ids[0:1, :], ids[1:2, :]], axis=1)
    rank = earlier_equal(assigned)
    kept = (assigned < expert_count) & (rank < CAP)
    return jnp.where(kept, assigned * CAP + rank, -1.0)


def regroup_phase(
    pos_ref,
    seg_ref,
    gain_ref,
    bias_ref,
    state_ref,
    query_ref,
    key_ref,
    value_ref,
    hidden_ref,
    out_rows,
    in_rows,
    out_offs,
    in_offs,
    send_sem,
    recv_sem,
    relay,
    relay_recv,
    relay_send,
    await_barrier,
):
    peers = lax.axis_size("dp")
    me = lax.axis_index("dp")
    tokens, width = state_ref.shape
    per_target = tokens // peers
    chunks = out_rows.shape[0]
    part = width // chunks
    both = 2 * tokens

    pos = pos_ref[...]
    target = (pos // tokens).astype(F32)
    offset = (pos % tokens).astype(F32)
    place = target * (2 * per_target) + earlier_equal(target)
    places = jnp.concatenate([place, place + per_target], axis=1).astype(jnp.int32)
    spread = (iota((both, both), 0) == places).astype(F32).astype(BF16)
    offset_column = as_column(offset)
    offset_both = jnp.concatenate([offset_column, offset_column + tokens], axis=0).astype(BF16)
    out_offs[...] = (
        jnp.dot(spread, offset_both, preferred_element_type=F32)
        .astype(BF16)
        .reshape(peers, 2 * per_target, tokens)
    )

    def fill(c):
        cols = pl.ds(pl.multiple_of(c * part, part), part)
        upper = jnp.concatenate([state_ref[:, cols], query_ref[:, cols]], axis=1)
        lower = jnp.concatenate([key_ref[:, cols], value_ref[:, cols]], axis=1)
        joined = jnp.concatenate([upper, lower], axis=0)
        out_rows[c] = (
            jnp.dot(spread, joined, preferred_element_type=F32)
            .astype(BF16)
            .reshape(peers, 2 * per_target, 2 * part)
        )

    def send_rows(c, to, frm):
        return pltpu.make_async_remote_copy(
            src_ref=out_rows.at[c, to],
            dst_ref=in_rows.at[c, frm],
            send_sem=send_sem.at[c, to],
            recv_sem=recv_sem.at[c, frm],
            device_id={"dp": to},
            device_id_type=MESH_ID,
        )

    def send_offs(to, frm):
        return pltpu.make_async_remote_copy(
            src_ref=out_offs.at[to],
            dst_ref=in_offs.at[frm],
            send_sem=send_sem.at[chunks, to],
            recv_sem=recv_sem.at[chunks, frm],
            device_id={"dp": to},
            device_id_type=MESH_ID,
        )

    def own_rows(c):
        return pltpu.make_async_copy(out_rows.at[c, me], in_rows.at[c, me], recv_sem.at[c, me])

    own_offs = pltpu.make_async_copy(out_offs.at[me], in_offs.at[me], recv_sem.at[chunks, me])

    chips = peers // 2
    z = me // 2
    core = me % 2
    opposite = chips // 2
    hop = opposite // 2

    def around(steps, on_core):
        return ((z + chips + steps) % chips) * 2 + on_core

    def to_relay(c, way):
        to = around(opposite, (way + core) % 2)
        return pltpu.make_async_remote_copy(
            src_ref=out_rows.at[c, to],
            dst_ref=relay.at[c, way],
            send_sem=send_sem.at[c, to],
            recv_sem=relay_recv.at[c, way],
            device_id={"dp": around(hop * (1 - 2 * way), core)},
            device_id_type=MESH_ID,
        )

    def forward(c, way):
        frm = around(-hop * (1 - 2 * way), core)
        return pltpu.make_async_remote_copy(
            src_ref=relay.at[c, way],
            dst_ref=in_rows.at[c, frm],
            send_sem=relay_send.at[c, way],
            recv_sem=recv_sem.at[c, frm],
            device_id={"dp": around(hop * (1 - 2 * way), (way + core) % 2)},
            device_id_type=MESH_ID,
        )

    def start_chunk(c, carry):
        def start_rows(k, inner):
            distance = opposite - 1 - k // 4
            steps = distance * (1 - 2 * (k % 2))
            send_rows(c, around(steps, (k // 2) % 2), me).start()
            return inner

        lax.fori_loop(0, 4 * (opposite - 1), start_rows, 0)
        send_rows(c, around(0, 1 - core), me).start()
        own_rows(c).start()
        return carry

    fill(0)
    await_barrier()
    own_offs.start()

    def start_offs(k, carry):
        send_offs((me + k) % peers, me).start()
        return carry

    lax.fori_loop(1, peers, start_offs, 0)

    def start_relays(c, carry):
        @pl.when(c > 0)
        def _():
            fill(c)

        for way in range(2):
            to_relay(c, way).start()

        @pl.when(c < ahead)
        def _():
            start_chunk(c, 0)

        return carry

    def pass_relays(c, carry):
        for way in range(2):
            to_relay(c, way).wait_recv()
            forward(c, way).start()
        return carry

    ahead = chunks // 2
    lax.fori_loop(0, chunks, start_relays, 0)
    lax.fori_loop(0, chunks, pass_relays, 0)
    lax.fori_loop(ahead, chunks, start_chunk, 0)

    segs = seg_ref[...].astype(F32)
    same_doc = as_column(segs) == jnp.broadcast_to(segs, (tokens, tokens))

    own_offs.wait()

    def await_offs(k, carry):
        send_offs(me, (me + k) % peers).wait_recv()
        return carry

    lax.fori_loop(1, peers, await_offs, 0)
    offs = in_offs[...].reshape(both, tokens).astype(F32)
    lanes = iota((both, tokens), 1).astype(F32)
    gather = jnp.concatenate([offs == lanes, offs == lanes + tokens], axis=1).astype(F32)
    gather = jnp.transpose(gather).astype(BF16)
    score_scale = 1.0 / math.sqrt(HEAD_DIM)

    def attend(c, carry):
        own_rows(c).wait()

        def await_rows(k, inner):
            send_rows(c, me, (me + k) % peers).wait_recv()
            return inner

        lax.fori_loop(1, peers, await_rows, 0)
        packed = jnp.dot(
            gather, in_rows[c].reshape(both, 2 * part), preferred_element_type=F32
        )
        states = packed[:tokens, :part]
        query = packed[:tokens, part:].astype(BF16)
        key = packed[tokens:, :part].astype(BF16)
        value = packed[tokens:, part:].astype(BF16)
        for h in range(part // HEAD_DIM):
            cols = slice(h * HEAD_DIM, (h + 1) * HEAD_DIM)
            scores = lax.dot_general(
                query[:, cols],
                key[:, cols],
                (((1,), (1,)), ((), ())),
                preferred_element_type=F32,
            )
            scores = jnp.where(same_doc, scores * score_scale, mask_fill)
            terms = jnp.exp(scores - jnp.max(scores, axis=1, keepdims=True))
            probs = (terms / jnp.sum(terms, axis=1, keepdims=True)).astype(BF16)
            mixed = jnp.dot(probs, value[:, cols], preferred_element_type=F32)
            at = pl.ds(pl.multiple_of(c * part + h * HEAD_DIM, HEAD_DIM), HEAD_DIM)
            hidden_ref[:, at] = states[:, cols] + mixed
        return carry

    lax.fori_loop(0, chunks, attend, 0)
    hidden = hidden_ref[...]
    centered = hidden - jnp.mean(hidden, axis=1, keepdims=True)
    variance = jnp.mean(centered * centered, axis=1, keepdims=True)
    normed = centered * lax.rsqrt(variance + epsilon) * gain_ref[...] + bias_ref[...]
    def drain(k, carry):
        peer = (me + k) % peers
        send_offs(peer, me).wait_send()

        def drain_chunk(c, inner):
            send_rows(c, peer, me).wait_send()
            return inner

        return lax.fori_loop(0, chunks, drain_chunk, carry)

    def drain_relays(c, carry):
        for way in range(2):
            forward(c, way).wait_send()
        return carry

    def drain_all():
        lax.fori_loop(1, peers, drain, 0)
        lax.fori_loop(0, chunks, drain_relays, 0)

    return normed.astype(BF16), drain_all


def expert_phase(
    b1_ref,
    b2_ref,
    loads,
    rows,
    part,
    pair_in,
    run_out,
    run_in,
    w1_v,
    w2_v,
    ag_send,
    ag_recv,
    sib_send,
    sib_recv,
    pair_send,
    pair_recv,
    run_send,
    run_recv,
):
    chips = lax.axis_size("dp") // 2
    me = lax.axis_index("dp")
    z = me // 2
    core = me % 2
    ahead = ((z + 1) % chips) * 2 + core
    behind = ((z + chips - 1) % chips) * 2 + core
    sibling = z * 2 + 1 - core
    half, width = rows.shape[3], rows.shape[4]
    steps = chips

    def pass_on(s, way):
        return pltpu.make_async_remote_copy(
            src_ref=rows.at[s, 0, way],
            dst_ref=rows.at[s + 1, 0, way],
            send_sem=ag_send.at[s, way],
            recv_sem=ag_recv.at[s, way],
            device_id={"dp": (ahead, behind)[way]},
            device_id_type=MESH_ID,
        )

    def to_sibling(s):
        return pltpu.make_async_remote_copy(
            src_ref=rows.at[s, 0],
            dst_ref=rows.at[s, 1],
            send_sem=sib_send.at[s],
            recv_sem=sib_recv.at[s],
            device_id={"dp": sibling},
            device_id_type=MESH_ID,
        )

    def pair(s):
        return pltpu.make_async_remote_copy(
            src_ref=part.at[s, 1],
            dst_ref=pair_in.at[s],
            send_sem=pair_send.at[s],
            recv_sem=pair_recv.at[s],
            device_id={"dp": sibling},
            device_id_type=MESH_ID,
        )

    def run(s, way):
        return pltpu.make_async_remote_copy(
            src_ref=run_out.at[s - 1, way],
            dst_ref=run_in.at[s - 1, way],
            send_sem=run_send.at[s - 1, way],
            recv_sem=run_recv.at[s - 1, way],
            device_id={"dp": (ahead, behind)[way]},
            device_id_type=MESH_ID,
        )

    def step(i, carry):
        @pl.when(i < steps)
        def _():
            @pl.when(i >= 1)
            def _():
                for way in range(2):
                    pass_on(i - 1, way).wait_recv()

            @pl.when(i < steps - 1)
            def _():
                for way in range(2):
                    pass_on(i, way).start()

            to_sibling(i).start()

        @pl.when(i == 1)
        def _():
            for load in loads:
                load.wait()

        @pl.when((i >= 1) & (i <= steps))
        def _():
            s = i - 1
            to_sibling(s).wait_recv()
            held = rows[s].reshape(4 * half, width)
            hidden = jnp.dot(held, w1_v[...], preferred_element_type=jnp.float32)
            hidden = jnp.maximum(hidden + b1_ref[...], 0.0).astype(jnp.bfloat16)
            share = jnp.dot(hidden, w2_v[...], preferred_element_type=jnp.float32)
            part[s] = share.astype(jnp.bfloat16).reshape(2, 2, half, width)
            pair(s).start()

        @pl.when(i == 3)
        def _():
            pair(1).wait_recv()
            total = part[1, 0].astype(jnp.float32) + pair_in[1].astype(jnp.float32)
            run_out[0] = total.astype(jnp.bfloat16)
            for way in range(2):
                run(1, way).start()

        @pl.when(i > 3)
        def _():
            s = i - 2
            pair(s).wait_recv()
            total = part[s, 0].astype(jnp.float32) + pair_in[s].astype(jnp.float32)
            for way in range(2):
                run(s - 1, way).wait_recv()
            total = total + run_in[s - 2].astype(jnp.float32)
            run_out[s - 1] = total.astype(jnp.bfloat16)
            for way in range(2):
                run(s, way).start()

        return carry

    lax.fori_loop(0, steps + 2, step, 0)
    pair(0).wait_recv()
    total = part[0, 0].astype(jnp.float32) + pair_in[0].astype(jnp.float32)
    total = total + b2_ref[pl.ds(lax.axis_index("expert"), 1), :].reshape(1, 1, width)
    for way in range(2):
        run(steps - 1, way).wait_recv()
    total = total + run_in[steps - 2].astype(jnp.float32)
    results = total.reshape(2 * half, width)

    def drain(s, carry):
        to_sibling(s).wait_send()
        pair(s).wait_send()

        @pl.when(s < steps - 1)
        def _():
            for way in range(2):
                pass_on(s, way).wait_send()
                run(s + 1, way).wait_send()

        return carry

    return results, lambda: lax.fori_loop(0, steps, drain, 0)


def exchange_phase(out_ref, in_ref, send_sem, recv_sem):
    peers = lax.axis_size("expert")
    me = lax.axis_index("expert")
    own = pltpu.make_async_copy(out_ref.at[me], in_ref.at[me], recv_sem.at[me])

    def move(to, frm):
        return pltpu.make_async_remote_copy(
            src_ref=out_ref.at[to],
            dst_ref=in_ref.at[frm],
            send_sem=send_sem.at[to],
            recv_sem=recv_sem.at[frm],
            device_id={"expert": to},
            device_id_type=MESH_ID,
        )

    def start(k, carry):
        move((me + k) % peers, me).start()
        return carry

    lax.fori_loop(1, peers, start, 0)
    own.start()
    own.wait()

    def finish(k, carry):
        move(me, (me + k) % peers).wait_recv()
        return carry

    lax.fori_loop(1, peers, finish, 0)

    def drain(k, carry):
        move((me + k) % peers, me).wait_send()
        return carry

    return lambda: lax.fori_loop(1, peers, drain, 0)


def layer_kernel(
    pos_ref,
    seg_ref,
    ids_ref,
    gate_ref,
    gain_ref,
    bias_ref,
    state_ref,
    query_ref,
    key_ref,
    value_ref,
    w1_ref,
    b1_ref,
    w2_ref,
    b2_ref,
    o_ref,
    hidden_ref,
    out_rows,
    in_rows,
    out_offs,
    in_offs,
    send_sem,
    recv_sem,
    relay,
    relay_recv,
    relay_send,
    stage,
    out_msgs,
    in_msgs,
    back_out,
    back_in,
    msg_send,
    msg_recv,
    load_sem,
    rows,
    part,
    pair_in,
    run_out,
    run_in,
    w1_v,
    w2_v,
    *ring_sems,
):
    dp_count = lax.axis_size("dp")
    expert_count = lax.axis_size("expert")
    dp_me = lax.axis_index("dp")
    expert_me = lax.axis_index("expert")
    tokens, width = state_ref.shape
    count = expert_count * CAP
    piece = stage.shape[2]
    pieces = stage.shape[1]
    loads = (
        pltpu.make_async_copy(w1_ref.at[0], w1_v, load_sem.at[0]),
        pltpu.make_async_copy(w2_ref.at[0], w2_v, load_sem.at[1]),
    )
    barrier = pltpu.get_barrier_semaphore()

    def greet_expert(k, carry):
        peer = (expert_me + k) % expert_count
        pl.semaphore_signal(barrier, inc=1, device_id={"expert": peer}, device_id_type=MESH_ID)
        return carry

    def greet_dp(k, carry):
        peer = (dp_me + k) % dp_count
        pl.semaphore_signal(barrier, inc=1, device_id={"dp": peer}, device_id_type=MESH_ID)
        return carry

    lax.fori_loop(1, expert_count, greet_expert, 0)
    lax.fori_loop(1, dp_count, greet_dp, 0)
    for load in loads:
        load.start()

    normed, drain_rows = regroup_phase(
        pos_ref,
        seg_ref,
        gain_ref,
        bias_ref,
        state_ref,
        query_ref,
        key_ref,
        value_ref,
        hidden_ref,
        out_rows,
        in_rows,
        out_offs,
        in_offs,
        send_sem,
        recv_sem,
        relay,
        relay_recv,
        relay_send,
        lambda: pl.semaphore_wait(barrier, dp_count + expert_count - 2),
    )

    def pack(ref):
        ref[...] = stage[...].reshape(ref.shape[0] * ref.shape[1], piece).astype(BF16).reshape(ref.shape)

    def unpack(ref):
        stage[...] = ref[...].reshape(ref.shape[0] * ref.shape[1], piece).astype(F32).reshape(stage.shape)

    slots = slot_row(ids_ref, expert_count)
    slot_hot = (iota((count, 2 * tokens), 0) == slots.astype(jnp.int32)).astype(F32)
    slot_hot = (slot_hot[:, :tokens] + slot_hot[:, tokens:]).astype(BF16)
    buffer = jnp.dot(slot_hot, normed, preferred_element_type=F32)
    for b in range(pieces):
        stage[:, b, :] = buffer[:, b * piece : (b + 1) * piece]
    pack(out_msgs)
    drain_out = exchange_phase(out_msgs, in_msgs, msg_send.at[0], msg_recv.at[0])
    unpack(in_msgs)
    half = count // 2
    for b in range(pieces):
        rows[0, 0, :, :, b * piece : (b + 1) * piece] = (
            stage[:, b, :].astype(BF16).reshape(2, half, piece)
        )
    results, drain_ring = expert_phase(
        b1_ref, b2_ref, loads, rows, part, pair_in, run_out, run_in, w1_v, w2_v, *ring_sems
    )
    for b in range(pieces):
        stage[:, b, :] = results[:, b * piece : (b + 1) * piece]
    pack(back_out)
    drain_back = exchange_phase(back_out, back_in, msg_send.at[1], msg_recv.at[1])
    unpack(back_in)

    gates = gate_ref[...].astype(F32) / 65536.0
    hots, weights = [], []
    for choice in range(2):
        column = as_column(slots[:, choice * tokens : (choice + 1) * tokens])
        hot = (column == iota((tokens, tokens), 1).astype(F32)).astype(F32).astype(BF16)
        hots.append(hot[:, :count])
        weights.append(as_column(gates[choice : choice + 1, :])[:, 0:1])
    for b in range(pieces):
        cols = slice(b * piece, (b + 1) * piece)
        returned = stage[:, b, :].astype(BF16)
        total = hidden_ref[:, cols]
        for hot, weight in zip(hots, weights):
            total = total + jnp.dot(hot, returned, preferred_element_type=F32) * weight
        o_ref[:, cols] = total.astype(BF16)
    drain_rows()
    drain_out()
    drain_ring()
    drain_back()


def per_device(
    pivot_states,
    queries,
    keys,
    values,
    pack_pos,
    segment_ids,
    expert_ids,
    gate_code,
    ln_gain,
    ln_bias,
    w_in,
    b_in,
    w_out,
    b_out,
):
    tokens, width = pivot_states.shape
    units = w_in.shape[2]
    peers = lax.axis_size("dp")
    expert_count = lax.axis_size("expert")
    count = expert_count * CAP
    half = count // 2
    chips = peers // 2
    chunks = 4
    group = 2 * tokens // peers
    pieces = 8
    piece = width // pieces
    dma = pltpu.SemaphoreType.DMA
    vmem = pl.BlockSpec(memory_space=pltpu.VMEM)
    any_space = pl.BlockSpec(memory_space=pl.ANY)
    messages = pltpu.VMEM((expert_count, CAP * pieces, piece), BF16)
    return pl.pallas_call(
        layer_kernel,
        out_shape=jax.ShapeDtypeStruct((tokens, width), BF16),
        in_specs=[vmem] * 10 + [any_space, vmem, any_space, vmem],
        out_specs=vmem,
        scratch_shapes=[
            pltpu.VMEM((tokens, width), F32),
            pltpu.VMEM((chunks, peers, group, 2 * width // chunks), BF16),
            pltpu.VMEM((chunks, peers, group, 2 * width // chunks), BF16),
            pltpu.VMEM((peers, group, tokens), BF16),
            pltpu.VMEM((peers, group, tokens), BF16),
            dma((chunks + 1, peers)),
            dma((chunks + 1, peers)),
            pltpu.VMEM((chunks, 2, group, 2 * width // chunks), BF16),
            dma((chunks, 2)),
            dma((chunks, 2)),
            pltpu.VMEM((count, pieces, piece), F32),
            messages,
            messages,
            messages,
            messages,
            dma((2, expert_count)),
            dma((2, expert_count)),
            dma((2,)),
            pltpu.VMEM((chips, 2, 2, half, width), BF16),
            pltpu.VMEM((chips, 2, 2, half, width), BF16),
            pltpu.VMEM((chips, 2, half, width), BF16),
            pltpu.VMEM((chips - 1, 2, half, width), BF16),
            pltpu.VMEM((chips - 1, 2, half, width), BF16),
            pltpu.VMEM((width, units), BF16),
            pltpu.VMEM((units, width), BF16),
            dma((chips - 1, 2)),
            dma((chips - 1, 2)),
            dma((chips,)),
            dma((chips,)),
            dma((chips,)),
            dma((chips,)),
            dma((chips - 1, 2)),
            dma((chips - 1, 2)),
        ],
        compiler_params=pltpu.CompilerParams(collective_id=1, has_side_effects=True),
        name="moe_layer",
    )(
        pack_pos[None, :],
        segment_ids,
        expert_ids.T,
        gate_code.T,
        ln_gain[None, :],
        ln_bias[None, :],
        pivot_states,
        queries,
        keys,
        values,
        w_in,
        b_in,
        w_out,
        b_out,
    )


def solution(mesh):
    return jax.shard_map(
        per_device,
        mesh=mesh,
        in_specs=(
            P(("dp", "expert"), None),
            P(("dp", "expert"), None),
            P(("dp", "expert"), None),
            P(("dp", "expert"), None),
            P(("dp", "expert")),
            P(("dp", "expert"), None),
            P(("dp", "expert"), None),
            P(("dp", "expert"), None),
            P(),
            P(),
            P("expert", None, "dp"),
            P("expert", "dp"),
            P("expert", "dp", None),
            P(),
        ),
        out_specs=P(("dp", "expert"), None),
        check_vma=False,
    )
```

```python
import math

import jax
import jax.numpy as jnp
from jax import lax
from jax.experimental import pallas as pl
from jax.experimental.pallas import tpu as pltpu
from jax.sharding import PartitionSpec as P

HEAD_DIM = 128
CAP = 2


epsilon = 1e-05
mask_fill = -1e30


MESH_ID = pl.DeviceIdType.MESH


F32 = jnp.float32
BF16 = jnp.bfloat16


def iota(shape, axis):
    return lax.broadcasted_iota(jnp.int32, shape, axis)


def as_column(row):
    count = row.shape[1]
    return jnp.transpose(jnp.broadcast_to(row, (count, count)))


def earlier_equal(row):
    count = row.shape[1]
    same = as_column(row) == jnp.broadcast_to(row, (count, count))
    before = iota((count, count), 0) < iota((count, count), 1)
    return jnp.sum((same & before).astype(F32), axis=0, keepdims=True)


def slot_row(ids_ref, expert_count):
    ids = ids_ref[...].astype(F32)
    assigned = jnp.concatenate([ids[0:1, :], ids[1:2, :]], axis=1)
    rank = earlier_equal(assigned)
    kept = (assigned < expert_count) & (rank < CAP)
    return jnp.where(kept, assigned * CAP + rank, -1.0)


def regroup_phase(
    pos_ref,
    seg_ref,
    gain_ref,
    bias_ref,
    state_ref,
    query_ref,
    key_ref,
    value_ref,
    hidden_ref,
    out_rows,
    in_rows,
    out_offs,
    in_offs,
    send_sem,
    recv_sem,
    relay,
    relay_recv,
    relay_send,
    await_barrier,
):
    peers = lax.axis_size("dp")
    me = lax.axis_index("dp")
    tokens, width = state_ref.shape
    per_target = tokens // peers
    chunks = out_rows.shape[0]
    part = width // chunks
    both = 2 * tokens

    pos = pos_ref[...]
    target = (pos // tokens).astype(F32)
    offset = (pos % tokens).astype(F32)
    place = target * (2 * per_target) + earlier_equal(target)
    places = jnp.concatenate([place, place + per_target], axis=1).astype(jnp.int32)
    spread = (iota((both, both), 0) == places).astype(F32).astype(BF16)
    offset_column = as_column(offset)
    offset_both = jnp.concatenate([offset_column, offset_column + tokens], axis=0).astype(BF16)
    out_offs[...] = (
        jnp.dot(spread, offset_both, preferred_element_type=F32)
        .astype(BF16)
        .reshape(peers, 2 * per_target, tokens)
    )

    def fill(c):
        cols = pl.ds(pl.multiple_of(c * part, part), part)
        upper = jnp.concatenate([state_ref[:, cols], query_ref[:, cols]], axis=1)
        lower = jnp.concatenate([key_ref[:, cols], value_ref[:, cols]], axis=1)
        joined = jnp.concatenate([upper, lower], axis=0)
        out_rows[c] = (
            jnp.dot(spread, joined, preferred_element_type=F32)
            .astype(BF16)
            .reshape(peers, 2 * per_target, 2 * part)
        )

    def send_rows(c, to, frm):
        return pltpu.make_async_remote_copy(
            src_ref=out_rows.at[c, to],
            dst_ref=in_rows.at[c, frm],
            send_sem=send_sem.at[c, to],
            recv_sem=recv_sem.at[c, frm],
            device_id={"dp": to},
            device_id_type=MESH_ID,
        )

    def send_offs(to, frm):
        return pltpu.make_async_remote_copy(
            src_ref=out_offs.at[to],
            dst_ref=in_offs.at[frm],
            send_sem=send_sem.at[chunks, to],
            recv_sem=recv_sem.at[chunks, frm],
            device_id={"dp": to},
            device_id_type=MESH_ID,
        )

    def own_rows(c):
        return pltpu.make_async_copy(out_rows.at[c, me], in_rows.at[c, me], recv_sem.at[c, me])

    own_offs = pltpu.make_async_copy(out_offs.at[me], in_offs.at[me], recv_sem.at[chunks, me])

    chips = peers // 2
    z = me // 2
    core = me % 2
    opposite = chips // 2
    hop = opposite // 2

    def around(steps, on_core):
        return ((z + chips + steps) % chips) * 2 + on_core

    def to_relay(c, way):
        to = around(opposite, (way + core) % 2)
        return pltpu.make_async_remote_copy(
            src_ref=out_rows.at[c, to],
            dst_ref=relay.at[c, way],
            send_sem=send_sem.at[c, to],
            recv_sem=relay_recv.at[c, way],
            device_id={"dp": around(hop * (1 - 2 * way), core)},
            device_id_type=MESH_ID,
        )

    def forward(c, way):
        frm = around(-hop * (1 - 2 * way), core)
        return pltpu.make_async_remote_copy(
            src_ref=relay.at[c, way],
            dst_ref=in_rows.at[c, frm],
            send_sem=relay_send.at[c, way],
            recv_sem=recv_sem.at[c, frm],
            device_id={"dp": around(hop * (1 - 2 * way), (way + core) % 2)},
            device_id_type=MESH_ID,
        )

    def start_chunk(c, carry):
        def start_rows(k, inner):
            distance = opposite - 1 - k // 4
            steps = distance * (1 - 2 * (k % 2))
            send_rows(c, around(steps, (k // 2) % 2), me).start()
            return inner

        lax.fori_loop(0, 4 * (opposite - 1), start_rows, 0)
        send_rows(c, around(0, 1 - core), me).start()
        own_rows(c).start()
        return carry

    fill(0)
    await_barrier()
    own_offs.start()

    def start_offs(k, carry):
        send_offs((me + k) % peers, me).start()
        return carry

    lax.fori_loop(1, peers, start_offs, 0)

    def start_relays(c, carry):
        @pl.when(c > 0)
        def _():
            fill(c)

        for way in range(2):
            to_relay(c, way).start()

        @pl.when(c < ahead)
        def _():
            start_chunk(c, 0)

        return carry

    def pass_relays(c, carry):
        for way in range(2):
            to_relay(c, way).wait_recv()
            forward(c, way).start()
        return carry

    ahead = chunks // 2
    lax.fori_loop(0, chunks, start_relays, 0)
    lax.fori_loop(0, chunks, pass_relays, 0)
    lax.fori_loop(ahead, chunks, start_chunk, 0)

    segs = seg_ref[...].astype(F32)
    same_doc = as_column(segs) == jnp.broadcast_to(segs, (tokens, tokens))

    own_offs.wait()

    def await_offs(k, carry):
        send_offs(me, (me + k) % peers).wait_recv()
        return carry

    lax.fori_loop(1, peers, await_offs, 0)
    offs = in_offs[...].reshape(both, tokens).astype(F32)
    lanes = iota((both, tokens), 1).astype(F32)
    gather = jnp.concatenate([offs == lanes, offs == lanes + tokens], axis=1).astype(F32)
    gather = jnp.transpose(gather).astype(BF16)
    score_scale = 1.0 / math.sqrt(HEAD_DIM)

    def attend(c, carry):
        own_rows(c).wait()

        def await_rows(k, inner):
            send_rows(c, me, (me + k) % peers).wait_recv()
            return inner

        lax.fori_loop(1, peers, await_rows, 0)
        packed = jnp.dot(
            gather, in_rows[c].reshape(both, 2 * part), preferred_element_type=F32
        )
        states = packed[:tokens, :part]
        query = packed[:tokens, part:].astype(BF16)
        key = packed[tokens:, :part].astype(BF16)
        value = packed[tokens:, part:].astype(BF16)
        for h in range(part // HEAD_DIM):
            cols = slice(h * HEAD_DIM, (h + 1) * HEAD_DIM)
            scores = lax.dot_general(
                query[:, cols],
                key[:, cols],
                (((1,), (1,)), ((), ())),
                preferred_element_type=F32,
            )
            scores = jnp.where(same_doc, scores * score_scale, mask_fill)
            terms = jnp.exp(scores - jnp.max(scores, axis=1, keepdims=True))
            probs = (terms / jnp.sum(terms, axis=1, keepdims=True)).astype(BF16)
            mixed = jnp.dot(probs, value[:, cols], preferred_element_type=F32)
            at = pl.ds(pl.multiple_of(c * part + h * HEAD_DIM, HEAD_DIM), HEAD_DIM)
            hidden_ref[:, at] = states[:, cols] + mixed
        return carry

    lax.fori_loop(0, chunks, attend, 0)
    hidden = hidden_ref[...]
    centered = hidden - jnp.mean(hidden, axis=1, keepdims=True)
    variance = jnp.mean(centered * centered, axis=1, keepdims=True)
    normed = centered * lax.rsqrt(variance + epsilon) * gain_ref[...] + bias_ref[...]
    def drain(k, carry):
        peer = (me + k) % peers
        send_offs(peer, me).wait_send()

        def drain_chunk(c, inner):
            send_rows(c, peer, me).wait_send()
            return inner

        return lax.fori_loop(0, chunks, drain_chunk, carry)

    def drain_relays(c, carry):
        for way in range(2):
            forward(c, way).wait_send()
        return carry

    def drain_all():
        lax.fori_loop(1, peers, drain, 0)
        lax.fori_loop(0, chunks, drain_relays, 0)

    return normed.astype(BF16), drain_all


def expert_phase(
    b1_ref,
    b2_ref,
    loads,
    rows,
    part,
    pair_in,
    run_out,
    run_in,
    w1_v,
    w2_v,
    ag_send,
    ag_recv,
    sib_send,
    sib_recv,
    pair_send,
    pair_recv,
    run_send,
    run_recv,
):
    chips = lax.axis_size("dp") // 2
    me = lax.axis_index("dp")
    z = me // 2
    core = me % 2
    ahead = ((z + 1) % chips) * 2 + core
    behind = ((z + chips - 1) % chips) * 2 + core
    sibling = z * 2 + 1 - core
    half, width = rows.shape[3], rows.shape[4]
    steps = chips

    quarter = half // 2
    lanes = [(way, sub) for sub in range(2) for way in range(2)]

    def pass_on(s, way, sub):
        at = pl.ds(sub * quarter, quarter)
        return pltpu.make_async_remote_copy(
            src_ref=rows.at[s, 0, way, at],
            dst_ref=rows.at[s + 1, 0, way, at],
            send_sem=ag_send.at[s, way, sub],
            recv_sem=ag_recv.at[s, way, sub],
            device_id={"dp": (ahead, behind)[way]},
            device_id_type=MESH_ID,
        )

    def to_sibling(s):
        return pltpu.make_async_remote_copy(
            src_ref=rows.at[s, 0],
            dst_ref=rows.at[s, 1],
            send_sem=sib_send.at[s],
            recv_sem=sib_recv.at[s],
            device_id={"dp": sibling},
            device_id_type=MESH_ID,
        )

    def pair(s):
        return pltpu.make_async_remote_copy(
            src_ref=part.at[s, 1],
            dst_ref=pair_in.at[s],
            send_sem=pair_send.at[s],
            recv_sem=pair_recv.at[s],
            device_id={"dp": sibling},
            device_id_type=MESH_ID,
        )

    def run(s, way, sub):
        at = pl.ds(sub * quarter, quarter)
        return pltpu.make_async_remote_copy(
            src_ref=run_out.at[s - 1, way, at],
            dst_ref=run_in.at[s - 1, way, at],
            send_sem=run_send.at[s - 1, way, sub],
            recv_sem=run_recv.at[s - 1, way, sub],
            device_id={"dp": (ahead, behind)[way]},
            device_id_type=MESH_ID,
        )

    def step(i, carry):
        @pl.when(i < steps)
        def _():
            for way, sub in lanes:

                @pl.when(i >= 1)
                def _():
                    pass_on(i - 1, way, sub).wait_recv()

                @pl.when(i < steps - 1)
                def _():
                    pass_on(i, way, sub).start()

            to_sibling(i).start()

        @pl.when(i == 1)
        def _():
            for load in loads:
                load.wait()

        @pl.when((i >= 1) & (i <= steps))
        def _():
            s = i - 1
            to_sibling(s).wait_recv()
            held = rows[s].reshape(4 * half, width)
            hidden = jnp.dot(held, w1_v[...], preferred_element_type=jnp.float32)
            hidden = jnp.maximum(hidden + b1_ref[...], 0.0).astype(jnp.bfloat16)
            share = jnp.dot(hidden, w2_v[...], preferred_element_type=jnp.float32)
            part[s] = share.astype(jnp.bfloat16).reshape(2, 2, half, width)
            pair(s).start()

        @pl.when(i == 3)
        def _():
            pair(1).wait_recv()
            total = part[1, 0].astype(jnp.float32) + pair_in[1].astype(jnp.float32)
            run_out[0] = total.astype(jnp.bfloat16)
            for way, sub in lanes:
                run(1, way, sub).start()

        @pl.when(i > 3)
        def _():
            s = i - 2
            pair(s).wait_recv()
            for way, sub in lanes:
                at = slice(sub * quarter, (sub + 1) * quarter)
                total = part[s, 0, way, at].astype(jnp.float32)
                total = total + pair_in[s, way, at].astype(jnp.float32)
                run(s - 1, way, sub).wait_recv()
                total = total + run_in[s - 2, way, at].astype(jnp.float32)
                run_out[s - 1, way, at] = total.astype(jnp.bfloat16)
                run(s, way, sub).start()

        return carry

    lax.fori_loop(0, steps + 2, step, 0)
    pair(0).wait_recv()
    total = part[0, 0].astype(jnp.float32) + pair_in[0].astype(jnp.float32)
    total = total + b2_ref[pl.ds(lax.axis_index("expert"), 1), :].reshape(1, 1, width)
    for way, sub in lanes:
        run(steps - 1, way, sub).wait_recv()
    total = total + run_in[steps - 2].astype(jnp.float32)
    results = total.reshape(2 * half, width)

    def drain(s, carry):
        to_sibling(s).wait_send()
        pair(s).wait_send()

        @pl.when(s < steps - 1)
        def _():
            for way, sub in lanes:
                pass_on(s, way, sub).wait_send()
                run(s + 1, way, sub).wait_send()

        return carry

    return results, lambda: lax.fori_loop(0, steps, drain, 0)


def exchange_phase(out_ref, in_ref, send_sem, recv_sem):
    peers = lax.axis_size("expert")
    me = lax.axis_index("expert")
    own = pltpu.make_async_copy(out_ref.at[me], in_ref.at[me], recv_sem.at[me])

    def move(to, frm):
        return pltpu.make_async_remote_copy(
            src_ref=out_ref.at[to],
            dst_ref=in_ref.at[frm],
            send_sem=send_sem.at[to],
            recv_sem=recv_sem.at[frm],
            device_id={"expert": to},
            device_id_type=MESH_ID,
        )

    def start(k, carry):
        move((me + k) % peers, me).start()
        return carry

    lax.fori_loop(1, peers, start, 0)
    own.start()
    own.wait()

    def finish(k, carry):
        move(me, (me + k) % peers).wait_recv()
        return carry

    lax.fori_loop(1, peers, finish, 0)

    def drain(k, carry):
        move((me + k) % peers, me).wait_send()
        return carry

    return lambda: lax.fori_loop(1, peers, drain, 0)


def layer_kernel(
    pos_ref,
    seg_ref,
    ids_ref,
    gate_ref,
    gain_ref,
    bias_ref,
    state_ref,
    query_ref,
    key_ref,
    value_ref,
    w1_ref,
    b1_ref,
    w2_ref,
    b2_ref,
    o_ref,
    hidden_ref,
    out_rows,
    in_rows,
    out_offs,
    in_offs,
    send_sem,
    recv_sem,
    relay,
    relay_recv,
    relay_send,
    stage,
    out_msgs,
    in_msgs,
    back_out,
    back_in,
    msg_send,
    msg_recv,
    load_sem,
    rows,
    part,
    pair_in,
    run_out,
    run_in,
    w1_v,
    w2_v,
    *ring_sems,
):
    dp_count = lax.axis_size("dp")
    expert_count = lax.axis_size("expert")
    dp_me = lax.axis_index("dp")
    expert_me = lax.axis_index("expert")
    tokens, width = state_ref.shape
    count = expert_count * CAP
    piece = stage.shape[2]
    pieces = stage.shape[1]
    loads = (
        pltpu.make_async_copy(w1_ref.at[0], w1_v, load_sem.at[0]),
        pltpu.make_async_copy(w2_ref.at[0], w2_v, load_sem.at[1]),
    )
    barrier = pltpu.get_barrier_semaphore()

    def greet_expert(k, carry):
        peer = (expert_me + k) % expert_count
        pl.semaphore_signal(barrier, inc=1, device_id={"expert": peer}, device_id_type=MESH_ID)
        return carry

    def greet_dp(k, carry):
        peer = (dp_me + k) % dp_count
        pl.semaphore_signal(barrier, inc=1, device_id={"dp": peer}, device_id_type=MESH_ID)
        return carry

    lax.fori_loop(1, expert_count, greet_expert, 0)
    lax.fori_loop(1, dp_count, greet_dp, 0)
    for load in loads:
        load.start()

    normed, drain_rows = regroup_phase(
        pos_ref,
        seg_ref,
        gain_ref,
        bias_ref,
        state_ref,
        query_ref,
        key_ref,
        value_ref,
        hidden_ref,
        out_rows,
        in_rows,
        out_offs,
        in_offs,
        send_sem,
        recv_sem,
        relay,
        relay_recv,
        relay_send,
        lambda: pl.semaphore_wait(barrier, dp_count + expert_count - 2),
    )

    def pack(ref):
        ref[...] = stage[...].reshape(ref.shape[0] * ref.shape[1], piece).astype(BF16).reshape(ref.shape)

    def unpack(ref):
        stage[...] = ref[...].reshape(ref.shape[0] * ref.shape[1], piece).astype(F32).reshape(stage.shape)

    slots = slot_row(ids_ref, expert_count)
    slot_hot = (iota((count, 2 * tokens), 0) == slots.astype(jnp.int32)).astype(F32)
    slot_hot = (slot_hot[:, :tokens] + slot_hot[:, tokens:]).astype(BF16)
    buffer = jnp.dot(slot_hot, normed, preferred_element_type=F32)
    for b in range(pieces):
        stage[:, b, :] = buffer[:, b * piece : (b + 1) * piece]
    pack(out_msgs)
    drain_out = exchange_phase(out_msgs, in_msgs, msg_send.at[0], msg_recv.at[0])
    unpack(in_msgs)
    half = count // 2
    for b in range(pieces):
        rows[0, 0, :, :, b * piece : (b + 1) * piece] = (
            stage[:, b, :].astype(BF16).reshape(2, half, piece)
        )
    results, drain_ring = expert_phase(
        b1_ref, b2_ref, loads, rows, part, pair_in, run_out, run_in, w1_v, w2_v, *ring_sems
    )
    for b in range(pieces):
        stage[:, b, :] = results[:, b * piece : (b + 1) * piece]
    pack(back_out)
    drain_back = exchange_phase(back_out, back_in, msg_send.at[1], msg_recv.at[1])
    unpack(back_in)

    gates = gate_ref[...].astype(F32) / 65536.0
    hots, weights = [], []
    for choice in range(2):
        column = as_column(slots[:, choice * tokens : (choice + 1) * tokens])
        hot = (column == iota((tokens, tokens), 1).astype(F32)).astype(F32).astype(BF16)
        hots.append(hot[:, :count])
        weights.append(as_column(gates[choice : choice + 1, :])[:, 0:1])
    for b in range(pieces):
        cols = slice(b * piece, (b + 1) * piece)
        returned = stage[:, b, :].astype(BF16)
        total = hidden_ref[:, cols]
        for hot, weight in zip(hots, weights):
            total = total + jnp.dot(hot, returned, preferred_element_type=F32) * weight
        o_ref[:, cols] = total.astype(BF16)
    drain_rows()
    drain_out()
    drain_ring()
    drain_back()


def per_device(
    pivot_states,
    queries,
    keys,
    values,
    pack_pos,
    segment_ids,
    expert_ids,
    gate_code,
    ln_gain,
    ln_bias,
    w_in,
    b_in,
    w_out,
    b_out,
):
    tokens, width = pivot_states.shape
    units = w_in.shape[2]
    peers = lax.axis_size("dp")
    expert_count = lax.axis_size("expert")
    count = expert_count * CAP
    half = count // 2
    chips = peers // 2
    chunks = 4
    group = 2 * tokens // peers
    pieces = 8
    piece = width // pieces
    dma = pltpu.SemaphoreType.DMA
    vmem = pl.BlockSpec(memory_space=pltpu.VMEM)
    any_space = pl.BlockSpec(memory_space=pl.ANY)
    messages = pltpu.VMEM((expert_count, CAP * pieces, piece), BF16)
    return pl.pallas_call(
        layer_kernel,
        out_shape=jax.ShapeDtypeStruct((tokens, width), BF16),
        in_specs=[vmem] * 10 + [any_space, vmem, any_space, vmem],
        out_specs=vmem,
        scratch_shapes=[
            pltpu.VMEM((tokens, width), F32),
            pltpu.VMEM((chunks, peers, group, 2 * width // chunks), BF16),
            pltpu.VMEM((chunks, peers, group, 2 * width // chunks), BF16),
            pltpu.VMEM((peers, group, tokens), BF16),
            pltpu.VMEM((peers, group, tokens), BF16),
            dma((chunks + 1, peers)),
            dma((chunks + 1, peers)),
            pltpu.VMEM((chunks, 2, group, 2 * width // chunks), BF16),
            dma((chunks, 2)),
            dma((chunks, 2)),
            pltpu.VMEM((count, pieces, piece), F32),
            messages,
            messages,
            messages,
            messages,
            dma((2, expert_count)),
            dma((2, expert_count)),
            dma((2,)),
            pltpu.VMEM((chips, 2, 2, half, width), BF16),
            pltpu.VMEM((chips, 2, 2, half, width), BF16),
            pltpu.VMEM((chips, 2, half, width), BF16),
            pltpu.VMEM((chips - 1, 2, half, width), BF16),
            pltpu.VMEM((chips - 1, 2, half, width), BF16),
            pltpu.VMEM((width, units), BF16),
            pltpu.VMEM((units, width), BF16),
            dma((chips - 1, 2, 2)),
            dma((chips - 1, 2, 2)),
            dma((chips,)),
            dma((chips,)),
            dma((chips,)),
            dma((chips,)),
            dma((chips - 1, 2, 2)),
            dma((chips - 1, 2, 2)),
        ],
        compiler_params=pltpu.CompilerParams(collective_id=1, has_side_effects=True),
        name="moe_layer",
    )(
        pack_pos[None, :],
        segment_ids,
        expert_ids.T,
        gate_code.T,
        ln_gain[None, :],
        ln_bias[None, :],
        pivot_states,
        queries,
        keys,
        values,
        w_in,
        b_in,
        w_out,
        b_out,
    )


def solution(mesh):
    return jax.shard_map(
        per_device,
        mesh=mesh,
        in_specs=(
            P(("dp", "expert"), None),
            P(("dp", "expert"), None),
            P(("dp", "expert"), None),
            P(("dp", "expert"), None),
            P(("dp", "expert")),
            P(("dp", "expert"), None),
            P(("dp", "expert"), None),
            P(("dp", "expert"), None),
            P(),
            P(),
            P("expert", None, "dp"),
            P("expert", "dp"),
            P("expert", "dp", None),
            P(),
        ),
        out_specs=P(("dp", "expert"), None),
        check_vma=False,
    )
```
